32 devices in a mesh: ctx: 8 (over z, core), tp: 4 (over y, x).
Axes of the slice: x: 2, y: 2, z: 4, core: 2. Of those that a mesh axis runs over, the one named last changes fastest.
Arguments:
- tokens: bfloat16 [4096, 4096], P(('ctx', 'tp')), may hold values from -6 to 6
- in_weight: bfloat16 [3, 4096, 2048], P(None, None, 'tp'), may hold values from -0.09375 to 0.09375
- short_taps: float32 [3, 3, 2048], P(None, None, 'tp'), may hold values from -3 to 3
- decay_rate: float32 [16, 2048], P(None, 'tp'), may hold values from 4.8828125e-05 to 0.0333333333
- residue: float32 [16, 2048], P(None, 'tp'), may hold values from -0.26 to 0.26
- skip_gain: float32 [2048], P('tp'), may hold values from -4 to 4
- grad_out: bfloat16 [4096, 2048], P('ctx', 'tp'), may hold values from -6 to 6
Outputs:
- mixed_out: bfloat16 [4096, 2048], P('ctx', 'tp')
- input_grad: bfloat16 [4096, 4096], P(('ctx', 'tp'))
The draws below stay inside these ranges and needn't reach their ends.
All inputs are finite; a program needn't handle non-finite values.
Results may differ from the reference program's by a relative error of at most 0.0065.
Values may be sent and summed in bfloat16 or wider, within the bound.
A program may use at most 192 MiB of HBM per device.

```python
import math
import jax
import jax.numpy as jnp
from jax import lax

D = 4096
CH = 2048
MODES = 16
SHORT = 3
TOKENS = 4096


def mode_table(key):
    folded = jax.random.fold_in(key, 11)
    subkeys = jax.random.split(folded, 4)
    fast_rate = jnp.exp(jax.random.uniform(subkeys[0], (MODES, CH), jnp.float32, math.log(1.0 / 50.0), math.log(1.0 / 30.0)))
    slow_rate = jnp.exp(jax.random.uniform(subkeys[1], (MODES, CH), jnp.float32, math.log(0.2 / TOKENS), math.log(2.0 / TOKENS)))
    fast_share = 0.5
    amplitude = jnp.clip(jax.random.normal(subkeys[3], (MODES, CH), jnp.float32), -4.0, 4.0)
    picked = jax.random.uniform(subkeys[2], (MODES, CH), jnp.float32) < fast_share
    decays = jnp.where(picked, fast_rate, slow_rate)
    weights = jnp.clip(amplitude * jnp.sqrt(2.0 * decays / MODES), -0.26, 0.26)
    return (decays, weights)


def draw_decay_rate(key, part):
    return mode_table(key)[0]


def draw_residue(key, part):
    return mode_table(key)[1]


def block_scale(own_key, shape, pieces, least, top_value):
    def one(dim, shards_of):
        steps = jax.random.uniform(jax.random.fold_in(jax.random.fold_in(own_key, 6), dim), (shards_of,), jnp.float32, least / len(pieces), top_value / len(pieces))
        return jnp.repeat(jnp.exp(steps), shape[dim] // shards_of).reshape((-1,) + (1,) * (len(shape) - dim - 1))

    factor_of = one(*pieces[0])
    for cut in pieces[1:]:
        factor_of = factor_of * one(*cut)
    return factor_of


def centred(stream_key, shape, scale, bound, shards=(), held_as=jnp.bfloat16):
    level = block_scale(stream_key, shape, shards, -0.22, 0.18) if shards else 1.0
    result = jax.random.normal(stream_key, shape, jnp.float32) * scale * level
    return jnp.minimum(jnp.maximum(result, -bound), bound).astype(held_as)


def setup_inputs(seed: int = 0) -> dict:
    keys = jax.random.split(jax.random.key(seed), 8)
    tokens = centred(keys[0], (TOKENS, D), 1.0, 6.0, ((0, 32),))
    in_weight = centred(keys[1], (3, D, CH), D ** -0.5, 0.09375, ((2, 4),))
    short_taps = centred(keys[2], (3, SHORT, CH), 0.6, 3.0, ((2, 4),), jnp.float32)
    decay_rate = draw_decay_rate(jax.random.fold_in(keys[7], 71), 0)
    residue = draw_residue(jax.random.fold_in(keys[7], 71), 0)
    skip_gain = centred(keys[5], (CH,), 1.0, 4.0, ((0, 4),), jnp.float32)
    grad_out = centred(keys[6], (TOKENS, CH), 1.0, 6.0, ((0, 8), (1, 4)))
    return {"tokens": tokens, "in_weight": in_weight, "short_taps": short_taps, "decay_rate": decay_rate, "residue": residue, "skip_gain": skip_gain, "grad_out": grad_out}


def reference(tokens, in_weight, short_taps, decay_rate, residue, skip_gain, grad_out):
    streams = jnp.stack([jnp.dot(tokens, in_weight[stream], preferred_element_type=jnp.float32).astype(jnp.bfloat16) for stream in range(3)], axis=1)
    tap_reach = SHORT - 1
    extended = jnp.concatenate([jnp.zeros((tap_reach, 3, CH), jnp.float32), streams.astype(jnp.float32)], axis=0)
    short_mixed = short_taps[:, 0][None] * extended[tap_reach:]
    for offset in range(1, tap_reach + 1):
        short_mixed = short_mixed + short_taps[:, offset][None] * extended[tap_reach - offset:tap_reach - offset + TOKENS]
    query_side = short_mixed[:, 0]
    key_side = short_mixed[:, 1]
    value_side = short_mixed[:, 2]
    product_in = key_side * value_side
    poles = jnp.exp(-decay_rate)

    def modal_step(state, column):
        state = poles * state + column[None]
        return state, jnp.sum(residue * state, axis=0)

    start_state = jnp.zeros((MODES, CH), jnp.float32)
    final_fwd, conv_out = lax.scan(modal_step, start_state, product_in)
    filtered = conv_out + skip_gain[None] * product_in
    mixed_out = (query_side * filtered).astype(jnp.bfloat16)
    upstream = grad_out.astype(jnp.float32)
    grad_query = upstream * filtered
    conv_grad = upstream * query_side
    final_bwd, back_conv = lax.scan(modal_step, start_state, conv_grad, reverse=True)
    grad_product = back_conv + skip_gain[None] * conv_grad
    stream_grads = jnp.stack([grad_query, grad_product * value_side, grad_product * key_side], axis=1)
    padded = jnp.concatenate([stream_grads, jnp.zeros((tap_reach, 3, CH), jnp.float32)], axis=0)
    grad_streams = short_taps[:, 0][None] * padded[:TOKENS]
    for offset in range(1, tap_reach + 1):
        grad_streams = grad_streams + short_taps[:, offset][None] * padded[offset:offset + TOKENS]
    grad_streams = grad_streams.astype(jnp.bfloat16)
    total = jnp.zeros((TOKENS, D), jnp.float32)
    for stream in range(3):
        total = total + jnp.dot(grad_streams[:, stream], in_weight[stream].T, preferred_element_type=jnp.float32)
    return mixed_out, total.astype(jnp.bfloat16)
```

```python
import functools

import jax
import jax.numpy as jnp
from jax import lax
from jax.experimental import pallas as pl
from jax.experimental.pallas import tpu as pltpu
from jax.sharding import PartitionSpec as P

exact_mode = lax.Precision.HIGHEST


def from_behind(value, axis, steps):
    count = lax.axis_size(axis)
    leading, last = (max(0, -steps), min(count, count - steps))
    return lax.ppermute(value, axis, [(source, source + steps) for source in range(leading, last)])


def modal_block(signal, log_pole, residue):
    length, channels = signal.shape
    sub_len = min(64, length)
    sub_count = length // sub_len
    offsets = jnp.arange(sub_len, dtype=jnp.float32)
    sections = signal.reshape(sub_count, sub_len, channels)
    powers = jnp.exp(log_pole[:, None, :] * offsets[None, :, None])
    filter_taps = jnp.sum(residue[:, None, :] * powers, axis=0)
    lag_index = jnp.arange(sub_len)[:, None] - jnp.arange(sub_len)[None, :]
    toeplitz = jnp.where((lag_index >= 0)[:, :, None], filter_taps[jnp.maximum(lag_index, 0)], 0.0)
    within = jnp.einsum("abc,kbc->kac", toeplitz, sections, precision=exact_mode)
    to_end = jnp.exp(log_pole[:, None, :] * (sub_len - 1.0 - offsets)[None, :, None])
    end_states = jnp.einsum("nbc,kbc->nkc", to_end, sections, precision=exact_mode)
    lag_blocks = jnp.arange(sub_count + 1)[:, None] - 1 - jnp.arange(sub_count)[None, :]
    valid_lag = lag_blocks >= 0
    lag_float = (jnp.maximum(lag_blocks, 0) * sub_len).astype(jnp.float32)
    decay_table = jnp.exp(log_pole[None, None] * lag_float[:, :, None, None])
    decay_table = jnp.where(valid_lag[:, :, None, None], decay_table, 0.0)
    carried = jnp.einsum("kmnc,nmc->nkc", decay_table, end_states, precision=exact_mode)
    stepped = residue[:, None, :] * jnp.exp(log_pole[:, None, :] * (offsets[None, :, None] + 1.0))
    output = within + jnp.einsum(
        "nac,nkc->kac", stepped, carried[:, :sub_count], precision=exact_mode
    )
    return (output.reshape(length, channels), carried[:, sub_count])


def carry_term(incoming, log_pole, residue, length):
    channels = incoming.shape[1]
    sub_len = min(64, length)
    sub_count = length // sub_len
    offsets = jnp.arange(sub_len, dtype=jnp.float32)
    stepped = residue[:, None, :] * jnp.exp(log_pole[:, None, :] * (offsets[None, :, None] + 1.0))
    block_starts = (jnp.arange(sub_count) * sub_len).astype(jnp.float32)
    start_states = incoming[:, None, :] * jnp.exp(
        log_pole[:, None, :] * block_starts[None, :, None]
    )
    output = jnp.einsum("nac,nkc->kac", stepped, start_states, precision=exact_mode)
    return output.reshape(length, channels)


def shards(tokens, in_weight, short_taps, decay_rate, residue, skip_gain, grad_out):
    width = in_weight.shape[2]
    weight_cat = jnp.concatenate([in_weight[0], in_weight[1], in_weight[2]], axis=1)
    streams = jnp.dot(
        lax.all_gather(tokens, "tp", axis=0, tiled=True),
        weight_cat,
        preferred_element_type=jnp.float32,
    ).astype(jnp.bfloat16)
    length = streams.shape[0]
    tap_reach = short_taps.shape[1] - 1
    taps_cat = jnp.concatenate([short_taps[0], short_taps[1], short_taps[2]], axis=1)
    before = from_behind(streams[length - tap_reach :], "ctx", 1)
    extended = jnp.concatenate([before, streams], axis=0).astype(jnp.float32)
    short_mixed = taps_cat[0][None] * extended[tap_reach:]
    for offset in range(1, tap_reach + 1):
        short_mixed = (
            short_mixed
            + taps_cat[offset][None] * extended[tap_reach - offset : tap_reach - offset + length]
        )
    query_side = short_mixed[:, :width]
    key_side = short_mixed[:, width : 2 * width]
    value_side = short_mixed[:, 2 * width :]
    product_in = key_side * value_side
    log_pole = -decay_rate
    forward_local, forward_sum = modal_block(product_in, log_pole, residue)
    upstream = grad_out.astype(jnp.float32)
    conv_grad = upstream * query_side
    backward_local, backward_sum = modal_block(conv_grad[::-1], log_pole, residue)
    position = lax.axis_index("ctx")
    summaries = (
        lax.all_gather(forward_sum[None], "ctx", axis=0, tiled=True),
        lax.all_gather(backward_sum[None], "ctx", axis=0, tiled=True),
    )
    block_index = jnp.arange(summaries[0].shape[0])
    earlier_gap = position - 1 - block_index
    later_gap = block_index - position - 1
    scale_fwd = (jnp.maximum(earlier_gap, 0) * length).astype(jnp.float32)
    scale_bwd = (jnp.maximum(later_gap, 0) * length).astype(jnp.float32)
    weight_fwd = jnp.where(
        (earlier_gap >= 0)[:, None, None], jnp.exp(log_pole[None] * scale_fwd[:, None, None]), 0.0
    )
    weight_bwd = jnp.where(
        (later_gap >= 0)[:, None, None], jnp.exp(log_pole[None] * scale_bwd[:, None, None]), 0.0
    )
    incoming_fwd = jnp.sum(weight_fwd * summaries[0], axis=0)
    incoming_bwd = jnp.sum(weight_bwd * summaries[1], axis=0)
    conv_out = forward_local + carry_term(incoming_fwd, log_pole, residue, length)
    back_conv = (backward_local + carry_term(incoming_bwd, log_pole, residue, length))[::-1]
    filtered = conv_out + skip_gain[None] * product_in
    result = (query_side * filtered).astype(jnp.bfloat16)
    grad_query = upstream * filtered
    grad_product = back_conv + skip_gain[None] * conv_grad
    stream_grads = jnp.concatenate(
        [grad_query, grad_product * value_side, grad_product * key_side], axis=1
    )
    after_rows = from_behind(stream_grads[:tap_reach], "ctx", -1)
    padded = jnp.concatenate([stream_grads, after_rows], axis=0)
    grad_streams = taps_cat[0][None] * padded[:length]
    for offset in range(1, tap_reach + 1):
        grad_streams = grad_streams + taps_cat[offset][None] * padded[offset : offset + length]
    grad_streams = grad_streams.astype(jnp.bfloat16)
    input_grad = lax.psum_scatter(
        jnp.einsum("rk,dk->rd", grad_streams, weight_cat, preferred_element_type=jnp.float32),
        "tp",
        scatter_dimension=0,
        tiled=True,
    )
    return (result, input_grad.astype(jnp.bfloat16))


MESH = pl.DeviceIdType.MESH
SUBLANES = 8
LANES = 128
ROWS = 32
TAIL = 16
VMEM_LIMIT = 60 * 1024 * 1024


def square_partners():
    me = lax.axis_index("tp")
    y, x = me // 2, me % 2
    return me, y * 2 + (1 - x), (1 - y) * 2 + x, (1 - y) * 2 + (1 - x)


def tree_sum(values):
    while len(values) > 1:
        values = [a + b for a, b in zip(values[::2], values[1::2])] + (
            [values[-1]] if len(values) % 2 else []
        )
    return values[0]


def fused_kernel(
    count, tok, w_hbm, taps, rate, res, skip, grad, mixed, out,
    w_buf, held, tails, acc, edge, side, prod, cgrad, conv, back, sgrad, gs, ghead, hrow,
    pole, dsec, dsub_f, dsub_b, gaps, carry_f, carry_b, end_f, end_b, in_f, in_b,
    mine_f, mine_b, all_f, all_b, inc_f, inc_b, out_buf, in_buf, own,
    w_sem, ag_send, ag_recv, nb_send, nb_recv, send_f, recv_f, send_b, recv_b, rs_send, rs_recv,
):
    f32, bf16 = jnp.float32, jnp.bfloat16
    rows, depth = tok.shape
    parts, _, tile = w_buf.shape
    width = grad.shape[1]
    length = grad.shape[0]
    modes = rate.shape[0]
    per_stream = width // tile
    section = rows // SUBLANES
    tiles = width // LANES
    tail, half, quarter, eighth = rows - TAIL, depth // 2, depth // 4, depth // 8
    me, xn, yn, dg = square_partners()
    pos = lax.axis_index("ctx")

    loads = []
    for part in range(parts):
        stream, col = divmod(part, per_stream)
        load = pltpu.make_async_copy(
            w_hbm.at[stream, :, pl.ds(col * tile, tile)], w_buf.at[part], w_sem.at[part]
        )
        load.start()
        loads.append(load)

    barrier = pltpu.get_barrier_semaphore()
    for partner in (xn, yn):
        pl.semaphore_signal(barrier, inc=1, device_id={"tp": partner}, device_id_type=MESH)
    for step in range(1, count):
        pl.semaphore_signal(
            barrier, inc=1, device_id={"ctx": lax.rem(pos + step, count)}, device_id_type=MESH
        )

    def gather(index, source, slot, row, row_count, col, col_count, partner):
        place = (pl.ds(row, row_count), pl.ds(col, col_count))
        return pltpu.make_async_remote_copy(
            src_ref=source.at[place],
            dst_ref=held.at[(slot,) + place],
            send_sem=ag_send.at[index],
            recv_sem=ag_recv.at[index],
            device_id={"tp": partner},
            device_id_type=MESH,
        )

    from_x, from_y = held.at[0], held.at[1]
    copies = [
        gather(0, tok, 0, tail, TAIL, 0, depth, xn),
        gather(1, tok, 1, tail, TAIL, 0, depth, yn),
        gather(2, tok, 0, 0, tail, half, eighth, xn),
        gather(3, tok, 1, 0, tail, 0, eighth, yn),
        gather(4, tok, 0, 0, tail, half + eighth, half - eighth, xn),
        gather(5, tok, 1, 0, tail, eighth, half - eighth, yn),
        gather(6, tok, 0, 0, tail, 0, quarter, xn),
        gather(7, tok, 1, 0, tail, half, quarter, yn),
        gather(8, tok, 0, 0, tail, quarter, quarter, xn),
        gather(9, tok, 1, 0, tail, half + quarter, quarter, yn),
        gather(10, from_y, 2, tail, TAIL, 0, half, xn),
        gather(11, from_x, 2, tail, TAIL, half, half, yn),
    ]
    cuts = [(i * eighth, eighth) for i in range(4)]
    for i, (start, size) in enumerate(cuts):
        copies.append(gather(12 + 2 * i, from_y, 2, 0, tail, start, size, xn))
        copies.append(gather(13 + 2 * i, from_x, 2, 0, tail, half + start, size, yn))

    def to_ctx(index, source, target, partner):
        return pltpu.make_async_remote_copy(
            src_ref=source,
            dst_ref=target,
            send_sem=nb_send.at[index],
            recv_sem=nb_recv.at[index],
            device_id={"ctx": partner},
            device_id_type=MESH,
        )

    after, prior = lax.rem(pos + 1, count), lax.rem(pos + count - 1, count)
    halo = to_ctx(0, edge.at[4], edge.at[0], after)
    side_head = to_ctx(
        1, side.at[:, pl.ds(0, 8), :], side.at[:, pl.ds(length, 8), :], prior
    )
    grad_head = to_ctx(2, grad.at[pl.ds(0, 16), :], ghead, prior)
    has_after, has_prior = pos < count - 1, pos > 0

    pl.semaphore_wait(barrier, 2 + count - 1)
    for index in range(4):
        copies[index].start()

    @pl.when(has_prior)
    def _():
        grad_head.start()

    @pl.when(jnp.logical_not(has_prior))
    def _():
        edge[0] = jnp.zeros((parts, 8, tile), f32)

    @pl.when(jnp.logical_not(has_after))
    def _():
        ghead[...] = jnp.zeros_like(ghead)
        side[:, pl.ds(length, 8), :] = jnp.zeros((3, 8, width), f32)

    pole[...] = jnp.exp(-rate[...])
    for index, steps in enumerate((section, 2 * section, 4 * section, rows)):
        dsec[index] = jnp.exp(rate[...] * (-1.0 * steps))
    sub = lax.broadcasted_iota(jnp.int32, (SUBLANES, LANES), 0)
    subf = lax.broadcasted_iota(jnp.int32, (SUBLANES, width), 0).astype(f32)

    @pl.loop(0, modes)
    def _(n):
        line = rate[pl.ds(n, 1), :]
        dsub_f[n] = jnp.exp(line * (subf * (-1.0 * section)))
        dsub_b[n] = jnp.exp(line * ((SUBLANES - 1.0 - subf) * (-1.0 * section)))

    @pl.loop(0, count)
    def _(g):
        gaps[g] = jnp.exp(rate[...] * (g * (-1 * length)).astype(f32))

    copies[0].wait_recv()
    copies[1].wait_recv()
    copies[10].start()
    copies[11].start()
    for index in range(4, 10):
        copies[index].start()

    def rounded(value):
        return value.astype(bf16).astype(f32)

    def multiply(slot, first, last, *ranges):
        @pl.loop(0, parts)
        def _(part):
            value = None
            for source, start, size in ranges:
                term = jnp.dot(
                    source[:, start : start + size],
                    w_buf[part, start : start + size, :],
                    preferred_element_type=f32,
                )
                value = term if value is None else value + term
            if not first:
                value = acc[slot, part, 8:, :] + value
            acc[slot, part, 8:, :] = rounded(value) if last else value

    for load in loads:
        load.wait()
    multiply(2, True, True, (tok, 0, depth))
    copies[10].wait_recv()
    copies[11].wait_recv()
    tails[0:TAIL] = tok[tail:, :]
    for slot in range(3):
        tails[(slot + 1) * TAIL : (slot + 2) * TAIL] = held[slot, tail:, :]

    @pl.loop(0, parts)
    def _(part):
        value = rounded(jnp.dot(tails[...], w_buf[part], preferred_element_type=f32))
        for slot, owner in enumerate((me, xn, yn, dg)):
            edge[owner + 1, part] = value[(slot + 1) * TAIL - 8 : (slot + 1) * TAIL]

    @pl.when(has_after)
    def _():
        halo.start()

    @pl.when(has_prior)
    def _():
        halo.wait_recv()

    def wide(ref, lanes):
        return [
            jnp.broadcast_to(ref[n : n + 1, lanes], (SUBLANES, LANES)) for n in range(modes)
        ]

    def process(slot, owner):
        base = pl.multiple_of(owner * rows, rows)
        acc[slot, :, 0:8, :] = edge[owner]

        @pl.loop(0, rows // ROWS)
        def _(step):
            start = pl.multiple_of(step * ROWS, ROWS)
            place = pl.ds(pl.multiple_of(base + start, ROWS), ROWS)
            for col in range(0, width, LANES):
                lanes = slice(col, col + LANES)
                mixed_side = []
                for s in range(3):
                    part, inner = s * per_stream + col // tile, col % tile
                    block = acc[slot, part, pl.ds(start, ROWS + 8), inner : inner + LANES]
                    value = taps[s, 0:1, lanes] * block[8:]
                    for j in range(1, 3):
                        value = value + taps[s, j : j + 1, lanes] * block[8 - j : 8 - j + ROWS]
                    side[s, place, lanes] = value
                    mixed_side.append(value)
                prod[col // LANES, place, :] = mixed_side[1] * mixed_side[2]
                cgrad[col // LANES, place, :] = grad[place, lanes].astype(f32) * mixed_side[0]

        @pl.when(jnp.logical_and(owner == 0, has_prior))
        def _():
            side_head.start()

        @pl.loop(0, tiles)
        def _(t):
            lanes = pl.ds(pl.multiple_of(t * LANES, LANES), LANES)
            p = wide(pole, lanes)

            def body(j, state):
                fwd, bwd = state
                x = prod[t, pl.ds(base + j, SUBLANES, stride=section), :]
                y = cgrad[t, pl.ds(base + (section - 1 - j), SUBLANES, stride=section), :]
                return (
                    [a * b + x for a, b in zip(p, fwd)],
                    [a * b + y for a, b in zip(p, bwd)],
                )

            zero = [jnp.zeros((SUBLANES, LANES), f32)] * modes
            fwd, bwd = lax.fori_loop(0, section, body, (zero, zero), unroll=2)
            for n in range(modes):
                residue = res[n : n + 1, lanes]
                ahead, behind = fwd[n] * residue, bwd[n] * residue
                for index, k in enumerate((1, 2, 4)):
                    decay = dsec[index, n : n + 1, lanes]
                    ahead = ahead + jnp.where(sub >= k, decay * pltpu.roll(ahead, k, 0), 0.0)
                    behind = behind + jnp.where(
                        sub < SUBLANES - k, decay * pltpu.roll(behind, SUBLANES - k, 0), 0.0
                    )
                carry_f[owner, n, :, lanes] = jnp.where(sub >= 1, pltpu.roll(ahead, 1, 0), 0.0)
                carry_b[owner, n, :, lanes] = jnp.where(
                    sub < SUBLANES - 1, pltpu.roll(behind, SUBLANES - 1, 0), 0.0
                )
                end_f[owner, n : n + 1, lanes] = ahead[SUBLANES - 1 :]
                end_b[owner, n : n + 1, lanes] = behind[0:1]

    process(2, me)
    copies[2].wait_recv()
    copies[4].wait_recv()
    for i in range(len(cuts)):
        copies[13 + 2 * i].start()
    copies[3].wait_recv()
    copies[5].wait_recv()
    for i in range(len(cuts)):
        copies[12 + 2 * i].start()
    multiply(0, True, False, (from_x, half, half))
    multiply(1, True, False, (from_y, 0, half))
    copies[6].wait_recv()
    multiply(0, False, False, (from_x, 0, quarter))
    copies[7].wait_recv()
    multiply(1, False, False, (from_y, half, quarter))
    copies[8].wait_recv()
    multiply(0, False, True, (from_x, quarter, quarter))
    process(0, xn)
    copies[9].wait_recv()
    multiply(1, False, True, (from_y, half + quarter, quarter))
    process(1, yn)
    opposite = held.at[2]
    for i, (start, size) in enumerate(cuts):
        copies[12 + 2 * i].wait_recv()
        copies[13 + 2 * i].wait_recv()
        multiply(
            2, i == 0, i == len(cuts) - 1, (opposite, start, size), (opposite, half + start, size)
        )
    process(2, dg)

    per_block = dsec[3]
    in_f[0] = jnp.zeros((modes, width), f32)
    in_b[3] = jnp.zeros((modes, width), f32)
    for block in range(4):
        in_f[block + 1] = per_block * in_f[block] + end_f[block]
    for block in (3, 2, 1):
        in_b[block - 1] = per_block * in_b[block] + end_b[block]
    mine_f[...] = in_f[4].astype(bf16)
    mine_b[...] = (per_block * in_b[0] + end_b[0]).astype(bf16)

    def summary(mine, table, send_sem, recv_sem, source, partner):
        return pltpu.make_async_remote_copy(
            src_ref=mine,
            dst_ref=table.at[source],
            send_sem=send_sem.at[partner],
            recv_sem=recv_sem.at[source],
            device_id={"ctx": partner},
            device_id_type=MESH,
        )

    forward = functools.partial(summary, mine_f, all_f, send_f, recv_f)
    backward = functools.partial(summary, mine_b, all_b, send_b, recv_b)
    for step in range(count):
        last = count - 1 - step

        @pl.when(last > pos)
        def _(last=last):
            forward(pos, last).start()

        @pl.when(step < pos)
        def _(step=step):
            backward(pos, step).start()

    @pl.when(has_after)
    def _():
        grad_head.wait_recv()
        side_head.wait_recv()

    inc_f[...] = jnp.zeros_like(inc_f)
    inc_b[...] = jnp.zeros_like(inc_b)
    for other in range(count):

        @pl.when(other < pos)
        def _(other=other):
            forward(other, pos).wait_recv()
            inc_f[...] += gaps[pos - 1 - other] * all_f[other].astype(f32)

        @pl.when(other > pos)
        def _(other=other):
            backward(other, pos).wait_recv()
            inc_b[...] += gaps[other - pos - 1] * all_b[other].astype(f32)

    arrived = inc_f[...]
    for block in range(5):
        in_f[block] = in_f[block] + arrived
        arrived = arrived * per_block
    arrived = inc_b[...]
    for block in (3, 2, 1, 0):
        in_b[block] = in_b[block] + arrived
        arrived = arrived * per_block

    def scan(base, owner, source, target, carry, incoming, shrink, reverse):
        @pl.loop(0, tiles)
        def _(t):
            lanes = pl.ds(pl.multiple_of(t * LANES, LANES), LANES)
            p, r = wide(pole, lanes), wide(res, lanes)

            def body(i, state):
                j = section - 1 - i if reverse else i
                place = pl.ds(base + j, SUBLANES, stride=section)
                x = source[t, place, :]
                state = [a * b + c * x for a, b, c in zip(p, state, r)]
                target[t, place, :] = tree_sum(state)
                return state

            start = [
                carry[owner, n, :, lanes]
                + shrink[n, :, lanes] * incoming[owner, n : n + 1, lanes]
                for n in range(modes)
            ]
            lax.fori_loop(0, section, body, start, unroll=2)

    def heads(owner):
        @pl.when(owner == 3)
        def _():
            hrow[...] = ghead[...].astype(f32)[0:8]

        @pl.when(owner < 3)
        def _():
            hrow[...] = grad[pl.ds(pl.multiple_of((owner + 1) * rows, rows), 16), :].astype(f32)[0:8]

        place = pl.ds(pl.multiple_of((owner + 1) * rows, rows), 8)
        for col in range(0, width, LANES):
            lanes = slice(col, col + LANES)
            q, k, v = (side[s, place, lanes] for s in range(3))
            g = hrow[:, lanes]
            x, cg = k * v, g * q
            p, r = pole[:, lanes], res[:, lanes]
            ahead, behind = p * in_f[owner + 1, :, lanes], in_b[owner, :, lanes]

            def total(value):
                return jnp.sum(value, axis=0, keepdims=True)

            first = sub == 0
            conv_head = jnp.where(first, total(ahead), total(p * ahead) + total(r * p) * x[0:1])
            conv_head = conv_head + total(r) * x
            back_head = jnp.where(
                first, total(behind), total(behind / p) - total(r / p) * cg[0:1]
            )
            gain = skip[0:1, lanes]
            filtered = conv_head + gain * x
            product = back_head + gain * cg
            for s, value in enumerate((g * filtered, product * v, product * k)):
                sgrad[rows:, s * width + col : s * width + col + LANES] = value

    def finish_block(owner):
        base = pl.multiple_of(owner * rows, rows)
        scan(base, owner, prod, conv, carry_f, in_f, dsub_f, False)
        scan(base, owner, cgrad, back, carry_b, in_b, dsub_b, True)
        heads(owner)

        @pl.loop(0, rows // ROWS)
        def _(step):
            start = pl.multiple_of(step * ROWS, ROWS)
            here = pl.ds(start, ROWS)
            place = pl.ds(pl.multiple_of(base + start, ROWS), ROWS)
            for col in range(0, width, LANES):
                lanes = slice(col, col + LANES)
                gain = skip[0:1, lanes]
                filtered = conv[col // LANES, place, :] + gain * prod[col // LANES, place, :]
                mixed[place, lanes] = (side[0, place, lanes] * filtered).astype(bf16)
                product = back[col // LANES, place, :] + gain * cgrad[col // LANES, place, :]
                upstream = grad[place, lanes].astype(f32)
                sgrad[here, lanes] = upstream * filtered
                sgrad[here, width + col : width + col + LANES] = product * side[2, place, lanes]
                sgrad[here, 2 * width + col : 2 * width + col + LANES] = (
                    product * side[1, place, lanes]
                )

        @pl.loop(0, rows // ROWS)
        def _(step):
            start = pl.multiple_of(step * ROWS, ROWS)
            place = pl.ds(pl.multiple_of(base + start, ROWS), ROWS)
            for s in range(3):
                for col in range(0, width, LANES):
                    lanes = slice(s * width + col, s * width + col + LANES)
                    block = sgrad[pl.ds(start, ROWS + 8), lanes]
                    value = taps[s, 0:1, col : col + LANES] * block[:ROWS]
                    for j in range(1, 3):
                        value = value + taps[s, j : j + 1, col : col + LANES] * block[j : j + ROWS]
                    gs[place, lanes] = value.astype(bf16)

    _, pieces, _, cols = out_buf.shape
    split = pieces // 2

    def send(kind, piece, partner):
        return pltpu.make_async_remote_copy(
            src_ref=out_buf.at[kind, piece],
            dst_ref=in_buf.at[kind, piece],
            send_sem=rs_send.at[kind, piece],
            recv_sem=rs_recv.at[kind, piece],
            device_id={"tp": partner},
            device_id_type=MESH,
        )

    def partial(owner, piece):
        block = pl.ds(pl.multiple_of(owner * rows, rows), rows)
        here = pl.ds(pl.multiple_of(piece * cols, cols), cols)
        total = None
        for part in range(parts):
            term = lax.dot_general(
                gs[block, part * tile : (part + 1) * tile],
                w_buf[part, here, :],
                (((1,), (1,)), ((), ())),
                preferred_element_type=f32,
            )
            total = term if total is None else total + term
        return total

    def emit(kind, piece, value, partner):
        out_buf[kind, piece] = value.astype(bf16)
        send(kind, piece, partner).start()

    finish_block(dg)

    @pl.loop(0, split)
    def _(k):
        emit(0, k, partial(dg, k), xn)
        emit(0, split + k, partial(dg, split + k), yn)

    finish_block(xn)
    finish_block(yn)

    @pl.loop(0, split)
    def _(k):
        emit(1, k, partial(xn, k), xn)
        emit(2, split + k, partial(yn, split + k), yn)

    @pl.loop(0, split)
    def _(k):
        own_x, own_y = partial(xn, split + k), partial(yn, k)
        send(0, split + k, yn).wait_recv()
        emit(1, split + k, own_x + in_buf[0, split + k].astype(f32), xn)
        send(0, k, xn).wait_recv()
        emit(2, k, own_y + in_buf[0, k].astype(f32), yn)

    finish_block(me)

    @pl.loop(0, pieces)
    def _(k):
        own[k] = partial(me, k)

    for k in [k + offset for k in range(split) for offset in (0, split)]:
        send(1, k, xn).wait_recv()
        send(2, k, yn).wait_recv()
        out[:, k * cols : (k + 1) * cols] = (
            own[k] + in_buf[1, k].astype(f32) + in_buf[2, k].astype(f32)
        ).astype(bf16)

    for copy in copies:
        copy.wait_send()
    for k in range(pieces):
        send(0, k, xn if k < split else yn).wait_send()
        send(1, k, xn).wait_send()
        send(2, k, yn).wait_send()

    @pl.when(has_after)
    def _():
        halo.wait_send()

    @pl.when(has_prior)
    def _():
        side_head.wait_send()
        grad_head.wait_send()

    for other in range(count):

        @pl.when(other > pos)
        def _(other=other):
            forward(pos, other).wait_send()

        @pl.when(other < pos)
        def _(other=other):
            backward(pos, other).wait_send()


def square_shards(tokens, in_weight, short_taps, decay_rate, residue, skip_gain, grad_out):
    count = lax.axis_size("ctx")
    rows, depth = tokens.shape
    streams, _, width = in_weight.shape
    length = 4 * rows
    modes = decay_rate.shape[0]
    tile = min(256, width)
    parts = streams * (width // tile)
    pieces = 8
    f32, bf16 = jnp.float32, jnp.bfloat16
    vmem, dma = pltpu.VMEM, pltpu.SemaphoreType.DMA
    table = vmem((modes, width), f32)
    plane = vmem((width // LANES, length, LANES), f32)
    fan = vmem((modes, SUBLANES, width), f32)
    carry = vmem((4, modes, SUBLANES, width), f32)
    ends = vmem((4, modes, width), f32)
    travelling = vmem((3, pieces, rows, depth // pieces), bf16)
    inner = pl.BlockSpec(memory_space=pltpu.VMEM)
    return pl.pallas_call(
        functools.partial(fused_kernel, count),
        out_shape=(
            jax.ShapeDtypeStruct((length, width), bf16),
            jax.ShapeDtypeStruct((rows, depth), bf16),
        ),
        in_specs=[inner, pl.BlockSpec(memory_space=pl.ANY)] + [inner] * 5,
        out_specs=(inner, inner),
        scratch_shapes=[
            vmem((parts, depth, tile), bf16),
            vmem((3, rows, depth), bf16),
            vmem((4 * TAIL, depth), bf16),
            vmem((3, parts, rows + 8, tile), f32),
            vmem((5, parts, 8, tile), f32),
            vmem((3, length + 8, width), f32),
            plane, plane, plane, plane,
            vmem((rows + 8, streams * width), f32),
            vmem((length, streams * width), bf16),
            vmem((16, width), bf16),
            vmem((8, width), f32),
            table,
            ends, fan, fan,
            vmem((count, modes, width), f32),
            carry, carry, ends, ends,
            vmem((5, modes, width), f32),
            ends,
            vmem((modes, width), bf16),
            vmem((modes, width), bf16),
            vmem((count, modes, width), bf16),
            vmem((count, modes, width), bf16),
            table, table,
            travelling, travelling,
            vmem((pieces, rows, depth // pieces), f32),
            dma((parts,)), dma((20,)), dma((20,)), dma((3,)), dma((3,)),
            dma((count,)), dma((count,)), dma((count,)), dma((count,)),
            dma((3, pieces)), dma((3, pieces)),
        ],
        compiler_params=pltpu.CompilerParams(
            collective_id=0, has_side_effects=True, vmem_limit_bytes=VMEM_LIMIT
        ),
    )(tokens, in_weight, short_taps, decay_rate, residue, skip_gain[None], grad_out)


def solution(mesh):
    in_specs = (
        P(("ctx", "tp"), None),
        P(None, None, "tp"),
        P(None, None, "tp"),
        P(None, "tp"),
        P(None, "tp"),
        P("tp"),
        P("ctx", "tp"),
    )
    out_specs = (P("ctx", "tp"), P(("ctx", "tp"), None))
    body = square_shards if mesh.shape["tp"] == 4 else shards
    return jax.shard_map(body, mesh=mesh, in_specs=in_specs, out_specs=out_specs, check_vma=False)
```

```python
import functools

import jax
import jax.numpy as jnp
from jax import lax
from jax.experimental import pallas as pl
from jax.experimental.pallas import tpu as pltpu
from jax.sharding import PartitionSpec as P

exact_mode = lax.Precision.HIGHEST


def from_behind(value, axis, steps):
    count = lax.axis_size(axis)
    leading, last = (max(0, -steps), min(count, count - steps))
    return lax.ppermute(value, axis, [(source, source + steps) for source in range(leading, last)])


def modal_block(signal, log_pole, residue):
    length, channels = signal.shape
    sub_len = min(64, length)
    sub_count = length // sub_len
    offsets = jnp.arange(sub_len, dtype=jnp.float32)
    sections = signal.reshape(sub_count, sub_len, channels)
    powers = jnp.exp(log_pole[:, None, :] * offsets[None, :, None])
    filter_taps = jnp.sum(residue[:, None, :] * powers, axis=0)
    lag_index = jnp.arange(sub_len)[:, None] - jnp.arange(sub_len)[None, :]
    toeplitz = jnp.where((lag_index >= 0)[:, :, None], filter_taps[jnp.maximum(lag_index, 0)], 0.0)
    within = jnp.einsum("abc,kbc->kac", toeplitz, sections, precision=exact_mode)
    to_end = jnp.exp(log_pole[:, None, :] * (sub_len - 1.0 - offsets)[None, :, None])
    end_states = jnp.einsum("nbc,kbc->nkc", to_end, sections, precision=exact_mode)
    lag_blocks = jnp.arange(sub_count + 1)[:, None] - 1 - jnp.arange(sub_count)[None, :]
    valid_lag = lag_blocks >= 0
    lag_float = (jnp.maximum(lag_blocks, 0) * sub_len).astype(jnp.float32)
    decay_table = jnp.exp(log_pole[None, None] * lag_float[:, :, None, None])
    decay_table = jnp.where(valid_lag[:, :, None, None], decay_table, 0.0)
    carried = jnp.einsum("kmnc,nmc->nkc", decay_table, end_states, precision=exact_mode)
    stepped = residue[:, None, :] * jnp.exp(log_pole[:, None, :] * (offsets[None, :, None] + 1.0))
    output = within + jnp.einsum(
        "nac,nkc->kac", stepped, carried[:, :sub_count], precision=exact_mode
    )
    return (output.reshape(length, channels), carried[:, sub_count])


def carry_term(incoming, log_pole, residue, length):
    channels = incoming.shape[1]
    sub_len = min(64, length)
    sub_count = length // sub_len
    offsets = jnp.arange(sub_len, dtype=jnp.float32)
    stepped = residue[:, None, :] * jnp.exp(log_pole[:, None, :] * (offsets[None, :, None] + 1.0))
    block_starts = (jnp.arange(sub_count) * sub_len).astype(jnp.float32)
    start_states = incoming[:, None, :] * jnp.exp(
        log_pole[:, None, :] * block_starts[None, :, None]
    )
    output = jnp.einsum("nac,nkc->kac", stepped, start_states, precision=exact_mode)
    return output.reshape(length, channels)


def shards(tokens, in_weight, short_taps, decay_rate, residue, skip_gain, grad_out):
    width = in_weight.shape[2]
    weight_cat = jnp.concatenate([in_weight[0], in_weight[1], in_weight[2]], axis=1)
    streams = jnp.dot(
        lax.all_gather(tokens, "tp", axis=0, tiled=True),
        weight_cat,
        preferred_element_type=jnp.float32,
    ).astype(jnp.bfloat16)
    length = streams.shape[0]
    tap_reach = short_taps.shape[1] - 1
    taps_cat = jnp.concatenate([short_taps[0], short_taps[1], short_taps[2]], axis=1)
    before = from_behind(streams[length - tap_reach :], "ctx", 1)
    extended = jnp.concatenate([before, streams], axis=0).astype(jnp.float32)
    short_mixed = taps_cat[0][None] * extended[tap_reach:]
    for offset in range(1, tap_reach + 1):
        short_mixed = (
            short_mixed
            + taps_cat[offset][None] * extended[tap_reach - offset : tap_reach - offset + length]
        )
    query_side = short_mixed[:, :width]
    key_side = short_mixed[:, width : 2 * width]
    value_side = short_mixed[:, 2 * width :]
    product_in = key_side * value_side
    log_pole = -decay_rate
    forward_local, forward_sum = modal_block(product_in, log_pole, residue)
    upstream = grad_out.astype(jnp.float32)
    conv_grad = upstream * query_side
    backward_local, backward_sum = modal_block(conv_grad[::-1], log_pole, residue)
    position = lax.axis_index("ctx")
    summaries = (
        lax.all_gather(forward_sum[None], "ctx", axis=0, tiled=True),
        lax.all_gather(backward_sum[None], "ctx", axis=0, tiled=True),
    )
    block_index = jnp.arange(summaries[0].shape[0])
    earlier_gap = position - 1 - block_index
    later_gap = block_index - position - 1
    scale_fwd = (jnp.maximum(earlier_gap, 0) * length).astype(jnp.float32)
    scale_bwd = (jnp.maximum(later_gap, 0) * length).astype(jnp.float32)
    weight_fwd = jnp.where(
        (earlier_gap >= 0)[:, None, None], jnp.exp(log_pole[None] * scale_fwd[:, None, None]), 0.0
    )
    weight_bwd = jnp.where(
        (later_gap >= 0)[:, None, None], jnp.exp(log_pole[None] * scale_bwd[:, None, None]), 0.0
    )
    incoming_fwd = jnp.sum(weight_fwd * summaries[0], axis=0)
    incoming_bwd = jnp.sum(weight_bwd * summaries[1], axis=0)
    conv_out = forward_local + carry_term(incoming_fwd, log_pole, residue, length)
    back_conv = (backward_local + carry_term(incoming_bwd, log_pole, residue, length))[::-1]
    filtered = conv_out + skip_gain[None] * product_in
    result = (query_side * filtered).astype(jnp.bfloat16)
    grad_query = upstream * filtered
    grad_product = back_conv + skip_gain[None] * conv_grad
    stream_grads = jnp.concatenate(
        [grad_query, grad_product * value_side, grad_product * key_side], axis=1
    )
    after_rows = from_behind(stream_grads[:tap_reach], "ctx", -1)
    padded = jnp.concatenate([stream_grads, after_rows], axis=0)
    grad_streams = taps_cat[0][None] * padded[:length]
    for offset in range(1, tap_reach + 1):
        grad_streams = grad_streams + taps_cat[offset][None] * padded[offset : offset + length]
    grad_streams = grad_streams.astype(jnp.bfloat16)
    input_grad = lax.psum_scatter(
        jnp.einsum("rk,dk->rd", grad_streams, weight_cat, preferred_element_type=jnp.float32),
        "tp",
        scatter_dimension=0,
        tiled=True,
    )
    return (result, input_grad.astype(jnp.bfloat16))


MESH = pl.DeviceIdType.MESH
SUBLANES = 8
LANES = 128
ROWS = 32
TAIL = 16
VMEM_LIMIT = 60 * 1024 * 1024


def square_partners():
    me = lax.axis_index("tp")
    y, x = me // 2, me % 2
    return me, y * 2 + (1 - x), (1 - y) * 2 + x, (1 - y) * 2 + (1 - x)


def tree_sum(values):
    while len(values) > 1:
        values = [a + b for a, b in zip(values[::2], values[1::2])] + (
            [values[-1]] if len(values) % 2 else []
        )
    return values[0]


def fused_kernel(
    count, tok_hbm, w_hbm, taps_hbm, rate_hbm, res_hbm, skip_hbm, grad_hbm, mixed, out,
    tok, taps, rate, res, skip, grad, w_buf, held, tails, acc, edge, side, prod, cgrad, conv, back, sgrad, gs, ghead, hrow,
    pole, dsec, dsub_f, dsub_b, gaps, carry_f, carry_b, end_f, end_b, in_f, in_b, new_f, new_b,
    mine_f, mine_b, all_f, all_b, inc_f, inc_b, out_buf, in_buf, own,
    in_sem, w_sem, ag_send, ag_recv, nb_send, nb_recv, send_f, recv_f, send_b, recv_b, rs_send, rs_recv,
):
    f32, bf16 = jnp.float32, jnp.bfloat16
    rows, depth = tok.shape
    parts, _, tile = w_buf.shape
    width = grad.shape[1]
    length = grad.shape[0]
    modes = rate.shape[0]
    per_stream = width // tile
    section = rows // SUBLANES
    tiles = width // LANES
    tail, half, quarter, eighth = rows - TAIL, depth // 2, depth // 4, depth // 8
    me, xn, yn, dg = square_partners()
    pos = lax.axis_index("ctx")

    barrier = pltpu.get_barrier_semaphore()
    for partner in (xn, yn):
        pl.semaphore_signal(barrier, inc=1, device_id={"tp": partner}, device_id_type=MESH)
    for step in range(1, count):
        pl.semaphore_signal(
            barrier, inc=1, device_id={"ctx": lax.rem(pos + step, count)}, device_id_type=MESH
        )

    pairs = (
        (rate_hbm, rate), (res_hbm, res), (taps_hbm, taps), (skip_hbm, skip),
        (tok_hbm, tok), (grad_hbm, grad),
    )
    inputs = [
        pltpu.make_async_copy(source, target, in_sem.at[index])
        for index, (source, target) in enumerate(pairs)
    ]
    for load in inputs:
        load.start()
    loads = []
    for part in range(parts):
        stream, col = divmod(part, per_stream)
        load = pltpu.make_async_copy(
            w_hbm.at[stream, :, pl.ds(col * tile, tile)], w_buf.at[part], w_sem.at[part]
        )
        load.start()
        loads.append(load)

    def gather(index, source, slot, row, row_count, col, col_count, partner):
        place = (pl.ds(row, row_count), pl.ds(col, col_count))
        return pltpu.make_async_remote_copy(
            src_ref=source.at[place],
            dst_ref=held.at[(slot,) + place],
            send_sem=ag_send.at[index],
            recv_sem=ag_recv.at[index],
            device_id={"tp": partner},
            device_id_type=MESH,
        )

    from_x, from_y = held.at[0], held.at[1]
    copies = [
        gather(0, tok_hbm, 0, tail, TAIL, 0, depth, xn),
        gather(1, tok_hbm, 1, tail, TAIL, 0, depth, yn),
        gather(2, tok_hbm, 0, 0, tail, half, eighth, xn),
        gather(3, tok_hbm, 1, 0, tail, 0, eighth, yn),
        gather(4, tok_hbm, 0, 0, tail, half + eighth, half - eighth, xn),
        gather(5, tok_hbm, 1, 0, tail, eighth, half - eighth, yn),
        gather(6, tok_hbm, 0, 0, tail, 0, quarter, xn),
        gather(7, tok_hbm, 1, 0, tail, half, quarter, yn),
        gather(8, tok_hbm, 0, 0, tail, quarter, quarter, xn),
        gather(9, tok_hbm, 1, 0, tail, half + quarter, quarter, yn),
        gather(10, from_y, 2, tail, TAIL, 0, half, xn),
        gather(11, from_x, 2, tail, TAIL, half, half, yn),
    ]
    sixteenth = eighth // 2
    cuts = [(0, 3 * sixteenth), (3 * sixteenth, eighth), (5 * sixteenth, eighth), (7 * sixteenth, sixteenth)]
    for i, (start, size) in enumerate(cuts):
        copies.append(gather(12 + 2 * i, from_y, 2, 0, tail, start, size, xn))
        copies.append(gather(13 + 2 * i, from_x, 2, 0, tail, half + start, size, yn))

    def to_ctx(index, source, target, partner):
        return pltpu.make_async_remote_copy(
            src_ref=source,
            dst_ref=target,
            send_sem=nb_send.at[index],
            recv_sem=nb_recv.at[index],
            device_id={"ctx": partner},
            device_id_type=MESH,
        )

    after, prior = lax.rem(pos + 1, count), lax.rem(pos + count - 1, count)
    halo = to_ctx(0, edge.at[4], edge.at[0], after)
    side_head = to_ctx(
        1, side.at[:, pl.ds(0, 8), :], side.at[:, pl.ds(length, 8), :], prior
    )
    grad_head = to_ctx(2, grad_hbm.at[pl.ds(0, 16), :], ghead, prior)
    has_after, has_prior = pos < count - 1, pos > 0

    pl.semaphore_wait(barrier, 2 + count - 1)
    for index in range(4):
        copies[index].start()

    @pl.when(has_prior)
    def _():
        grad_head.start()

    @pl.when(jnp.logical_not(has_prior))
    def _():
        edge[0] = jnp.zeros((parts, 8, tile), f32)

    @pl.when(jnp.logical_not(has_after))
    def _():
        ghead[...] = jnp.zeros_like(ghead)
        side[:, pl.ds(length, 8), :] = jnp.zeros((3, 8, width), f32)

    for load in inputs:
        load.wait()
    pole[...] = jnp.exp(-rate[...])
    for index, steps in enumerate((section, 2 * section, 4 * section, rows)):
        dsec[index] = jnp.exp(rate[...] * (-1.0 * steps))
    sub = lax.broadcasted_iota(jnp.int32, (SUBLANES, LANES), 0)
    subf = lax.broadcasted_iota(jnp.int32, (SUBLANES, width), 0).astype(f32)

    @pl.loop(0, modes)
    def _(n):
        line = rate[pl.ds(n, 1), :]
        dsub_f[n] = jnp.exp(line * (subf * (-1.0 * section)))
        dsub_b[n] = jnp.exp(line * ((SUBLANES - 1.0 - subf) * (-1.0 * section)))

    @pl.loop(0, count)
    def _(g):
        gaps[g] = jnp.exp(rate[...] * (g * (-1 * length)).astype(f32))

    copies[0].wait_recv()
    copies[1].wait_recv()
    copies[10].start()
    copies[11].start()
    for index in range(4, 10):
        copies[index].start()

    def rounded(value):
        return value.astype(bf16).astype(f32)

    def multiply(slot, first, last, *ranges):
        @pl.loop(0, parts)
        def _(part):
            value = None
            for source, start, size in ranges:
                term = jnp.dot(
                    source[:, start : start + size],
                    w_buf[part, start : start + size, :],
                    preferred_element_type=f32,
                )
                value = term if value is None else value + term
            if not first:
                value = acc[slot, part, 8:, :] + value
            acc[slot, part, 8:, :] = rounded(value) if last else value

    for load in loads:
        load.wait()
    multiply(2, True, True, (tok, 0, depth))
    copies[10].wait_recv()
    copies[11].wait_recv()
    tails[0:TAIL] = tok[tail:, :]
    for slot in range(3):
        tails[(slot + 1) * TAIL : (slot + 2) * TAIL] = held[slot, tail:, :]

    @pl.loop(0, parts)
    def _(part):
        value = rounded(jnp.dot(tails[...], w_buf[part], preferred_element_type=f32))
        for slot, owner in enumerate((me, xn, yn, dg)):
            edge[owner + 1, part] = value[(slot + 1) * TAIL - 8 : (slot + 1) * TAIL]

    @pl.when(has_after)
    def _():
        halo.start()

    @pl.when(has_prior)
    def _():
        halo.wait_recv()

    def wide(ref, lanes):
        return [
            jnp.broadcast_to(ref[n : n + 1, lanes], (SUBLANES, LANES)) for n in range(modes)
        ]

    def process(slot, owner):
        base = pl.multiple_of(owner * rows, rows)
        acc[slot, :, 0:8, :] = edge[owner]

        @pl.loop(0, rows // ROWS)
        def _(step):
            start = pl.multiple_of(step * ROWS, ROWS)
            place = pl.ds(pl.multiple_of(base + start, ROWS), ROWS)
            for col in range(0, width, LANES):
                lanes = slice(col, col + LANES)
                mixed_side = []
                for s in range(3):
                    part, inner = s * per_stream + col // tile, col % tile
                    block = acc[slot, part, pl.ds(start, ROWS + 8), inner : inner + LANES]
                    value = taps[s, 0:1, lanes] * block[8:]
                    for j in range(1, 3):
                        value = value + taps[s, j : j + 1, lanes] * block[8 - j : 8 - j + ROWS]
                    side[s, place, lanes] = value
                    mixed_side.append(value)
                prod[col // LANES, place, :] = mixed_side[1] * mixed_side[2]
                cgrad[col // LANES, place, :] = grad[place, lanes].astype(f32) * mixed_side[0]

        @pl.when(jnp.logical_and(owner == 0, has_prior))
        def _():
            side_head.start()

        @pl.loop(0, tiles)
        def _(t):
            lanes = pl.ds(pl.multiple_of(t * LANES, LANES), LANES)
            p = wide(pole, lanes)

            def body(j, state):
                fwd, bwd = state
                x = prod[t, pl.ds(base + j, SUBLANES, stride=section), :]
                y = cgrad[t, pl.ds(base + (section - 1 - j), SUBLANES, stride=section), :]
                return (
                    [a * b + x for a, b in zip(p, fwd)],
                    [a * b + y for a, b in zip(p, bwd)],
                )

            zero = [jnp.zeros((SUBLANES, LANES), f32)] * modes
            fwd, bwd = lax.fori_loop(0, section, body, (zero, zero), unroll=2)
            for n in range(modes):
                residue = res[n : n + 1, lanes]
                ahead, behind = fwd[n] * residue, bwd[n] * residue
                for index, k in enumerate((1, 2, 4)):
                    decay = dsec[index, n : n + 1, lanes]
                    ahead = ahead + jnp.where(sub >= k, decay * pltpu.roll(ahead, k, 0), 0.0)
                    behind = behind + jnp.where(
                        sub < SUBLANES - k, decay * pltpu.roll(behind, SUBLANES - k, 0), 0.0
                    )
                carry_f[owner, n, :, lanes] = jnp.where(sub >= 1, pltpu.roll(ahead, 1, 0), 0.0)
                carry_b[owner, n, :, lanes] = jnp.where(
                    sub < SUBLANES - 1, pltpu.roll(behind, SUBLANES - 1, 0), 0.0
                )
                end_f[owner, n : n + 1, lanes] = ahead[SUBLANES - 1 :]
                end_b[owner, n : n + 1, lanes] = behind[0:1]

    def scan(base, owner, source, target, carry, incoming, shrink, reverse):
        @pl.loop(0, tiles)
        def _(t):
            lanes = pl.ds(pl.multiple_of(t * LANES, LANES), LANES)
            p, r = wide(pole, lanes), wide(res, lanes)

            def body(i, state):
                j = section - 1 - i if reverse else i
                place = pl.ds(base + j, SUBLANES, stride=section)
                x = source[t, place, :]
                state = [a * b + c * x for a, b, c in zip(p, state, r)]
                target[t, place, :] = tree_sum(state)
                return state

            start = [
                carry[owner, n, :, lanes]
                + shrink[n, :, lanes] * incoming[owner, n : n + 1, lanes]
                for n in range(modes)
            ]
            lax.fori_loop(0, section, body, start, unroll=2)

    def finish_scan(owner):
        base = pl.multiple_of(owner * rows, rows)
        scan(base, owner, prod, conv, carry_f, in_f, dsub_f, False)
        scan(base, owner, cgrad, back, carry_b, in_b, dsub_b, True)

    def add_arrived(owner, target, incoming, shrink, reverse):
        base = pl.multiple_of(owner * rows, rows)

        @pl.loop(0, tiles)
        def _(t):
            lanes = pl.ds(pl.multiple_of(t * LANES, LANES), LANES)
            p = wide(pole, lanes)

            def body(i, state):
                j = section - 1 - i if reverse else i
                place = pl.ds(base + j, SUBLANES, stride=section)
                state = [a * b for a, b in zip(p, state)]
                target[t, place, :] = target[t, place, :] + tree_sum(state)
                return state

            start = [
                shrink[n, :, lanes] * incoming[owner, n : n + 1, lanes] for n in range(modes)
            ]
            lax.fori_loop(0, section, body, start, unroll=2)

    process(2, me)
    copies[2].wait_recv()
    copies[4].wait_recv()
    for i in range(len(cuts)):
        copies[13 + 2 * i].start()
    copies[3].wait_recv()
    copies[5].wait_recv()
    for i in range(len(cuts)):
        copies[12 + 2 * i].start()
    multiply(0, True, False, (from_x, half, half))
    multiply(1, True, False, (from_y, 0, half))
    copies[6].wait_recv()
    multiply(0, False, False, (from_x, 0, quarter))
    copies[7].wait_recv()
    multiply(1, False, False, (from_y, half, quarter))
    copies[8].wait_recv()
    multiply(0, False, True, (from_x, quarter, quarter))
    process(0, xn)
    copies[9].wait_recv()
    multiply(1, False, True, (from_y, half + quarter, quarter))
    process(1, yn)
    opposite = held.at[2]
    for i, (start, size) in enumerate(cuts):
        copies[12 + 2 * i].wait_recv()
        copies[13 + 2 * i].wait_recv()
        multiply(
            2, i == 0, i == len(cuts) - 1, (opposite, start, size), (opposite, half + start, size)
        )
    process(2, dg)

    per_block = dsec[3]
    in_f[0] = jnp.zeros((modes, width), f32)
    in_b[3] = jnp.zeros((modes, width), f32)
    for block in range(4):
        in_f[block + 1] = per_block * in_f[block] + end_f[block]
    for block in (3, 2, 1):
        in_b[block - 1] = per_block * in_b[block] + end_b[block]
    mine_f[...] = in_f[4].astype(bf16)
    mine_b[...] = (per_block * in_b[0] + end_b[0]).astype(bf16)

    def summary(mine, table, send_sem, recv_sem, source, partner):
        return pltpu.make_async_remote_copy(
            src_ref=mine,
            dst_ref=table.at[source],
            send_sem=send_sem.at[partner],
            recv_sem=recv_sem.at[source],
            device_id={"ctx": partner},
            device_id_type=MESH,
        )

    forward = functools.partial(summary, mine_f, all_f, send_f, recv_f)
    backward = functools.partial(summary, mine_b, all_b, send_b, recv_b)
    for step in range(count):
        last = count - 1 - step

        @pl.when(last > pos)
        def _(last=last):
            forward(pos, last).start()

        @pl.when(step < pos)
        def _(step=step):
            backward(pos, step).start()

    finish_scan(dg)

    @pl.when(has_after)
    def _():
        grad_head.wait_recv()
        side_head.wait_recv()

    inc_f[...] = jnp.zeros_like(inc_f)
    inc_b[...] = jnp.zeros_like(inc_b)
    for other in range(count):

        @pl.when(other < pos)
        def _(other=other):
            forward(other, pos).wait_recv()
            inc_f[...] += gaps[pos - 1 - other] * all_f[other].astype(f32)

        @pl.when(other > pos)
        def _(other=other):
            backward(other, pos).wait_recv()
            inc_b[...] += gaps[other - pos - 1] * all_b[other].astype(f32)

    arrived = inc_f[...]
    for block in range(5):
        in_f[block] = in_f[block] + arrived
        new_f[block] = arrived
        arrived = arrived * per_block
    arrived = inc_b[...]
    for block in (3, 2, 1, 0):
        in_b[block] = in_b[block] + arrived
        new_b[block] = arrived
        arrived = arrived * per_block
    add_arrived(dg, conv, new_f, dsub_f, False)
    add_arrived(dg, back, new_b, dsub_b, True)

    def heads(owner):
        @pl.when(owner == 3)
        def _():
            hrow[...] = ghead[...].astype(f32)[0:8]

        @pl.when(owner < 3)
        def _():
            hrow[...] = grad[pl.ds(pl.multiple_of((owner + 1) * rows, rows), 16), :].astype(f32)[0:8]

        place = pl.ds(pl.multiple_of((owner + 1) * rows, rows), 8)
        for col in range(0, width, LANES):
            lanes = slice(col, col + LANES)
            q, k, v = (side[s, place, lanes] for s in range(3))
            g = hrow[:, lanes]
            x, cg = k * v, g * q
            p, r = pole[:, lanes], res[:, lanes]
            ahead, behind = p * in_f[owner + 1, :, lanes], in_b[owner, :, lanes]

            def total(value):
                return jnp.sum(value, axis=0, keepdims=True)

            first = sub == 0
            conv_head = jnp.where(first, total(ahead), total(p * ahead) + total(r * p) * x[0:1])
            conv_head = conv_head + total(r) * x
            back_head = jnp.where(
                first, total(behind), total(behind / p) - total(r / p) * cg[0:1]
            )
            gain = skip[0:1, lanes]
            filtered = conv_head + gain * x
            product = back_head + gain * cg
            for s, value in enumerate((g * filtered, product * v, product * k)):
                sgrad[rows:, s * width + col : s * width + col + LANES] = value

    def finish_block(owner):
        base = pl.multiple_of(owner * rows, rows)
        heads(owner)

        @pl.loop(0, rows // ROWS)
        def _(step):
            start = pl.multiple_of(step * ROWS, ROWS)
            here = pl.ds(start, ROWS)
            place = pl.ds(pl.multiple_of(base + start, ROWS), ROWS)
            for col in range(0, width, LANES):
                lanes = slice(col, col + LANES)
                gain = skip[0:1, lanes]
                filtered = conv[col // LANES, place, :] + gain * prod[col // LANES, place, :]
                mixed[place, lanes] = (side[0, place, lanes] * filtered).astype(bf16)
                product = back[col // LANES, place, :] + gain * cgrad[col // LANES, place, :]
                upstream = grad[place, lanes].astype(f32)
                sgrad[here, lanes] = upstream * filtered
                sgrad[here, width + col : width + col + LANES] = product * side[2, place, lanes]
                sgrad[here, 2 * width + col : 2 * width + col + LANES] = (
                    product * side[1, place, lanes]
                )

        @pl.loop(0, rows // ROWS)
        def _(step):
            start = pl.multiple_of(step * ROWS, ROWS)
            place = pl.ds(pl.multiple_of(base + start, ROWS), ROWS)
            for s in range(3):
                for col in range(0, width, LANES):
                    lanes = slice(s * width + col, s * width + col + LANES)
                    block = sgrad[pl.ds(start, ROWS + 8), lanes]
                    value = taps[s, 0:1, col : col + LANES] * block[:ROWS]
                    for j in range(1, 3):
                        value = value + taps[s, j : j + 1, col : col + LANES] * block[j : j + ROWS]
                    gs[place, lanes] = value.astype(bf16)

    _, pieces, _, cols = out_buf.shape
    split = pieces // 2

    def send(kind, piece, partner):
        return pltpu.make_async_remote_copy(
            src_ref=out_buf.at[kind, piece],
            dst_ref=in_buf.at[kind, piece],
            send_sem=rs_send.at[kind, piece],
            recv_sem=rs_recv.at[kind, piece],
            device_id={"tp": partner},
            device_id_type=MESH,
        )

    def partial(owner, piece):
        block = pl.ds(pl.multiple_of(owner * rows, rows), rows)
        here = pl.ds(pl.multiple_of(piece * cols, cols), cols)
        total = None
        for part in range(parts):
            term = lax.dot_general(
                gs[block, part * tile : (part + 1) * tile],
                w_buf[part, here, :],
                (((1,), (1,)), ((), ())),
                preferred_element_type=f32,
            )
            total = term if total is None else total + term
        return total

    def emit(kind, piece, value, partner):
        out_buf[kind, piece] = value.astype(bf16)
        send(kind, piece, partner).start()

    finish_block(dg)

    @pl.loop(0, split)
    def _(k):
        emit(0, k, partial(dg, k), xn)
        emit(0, split + k, partial(dg, split + k), yn)

    finish_scan(xn)
    finish_block(xn)
    finish_scan(yn)
    finish_block(yn)

    @pl.loop(0, split)
    def _(k):
        emit(1, k, partial(xn, k), xn)
        emit(2, split + k, partial(yn, split + k), yn)

    @pl.loop(0, split)
    def _(k):
        own_x, own_y = partial(xn, split + k), partial(yn, k)
        send(0, split + k, yn).wait_recv()
        emit(1, split + k, own_x + in_buf[0, split + k].astype(f32), xn)
        send(0, k, xn).wait_recv()
        emit(2, k, own_y + in_buf[0, k].astype(f32), yn)

    finish_scan(me)
    finish_block(me)

    @pl.loop(0, pieces)
    def _(k):
        own[k] = partial(me, k)

    for k in [k + offset for k in range(split) for offset in (0, split)]:
        send(1, k, xn).wait_recv()
        send(2, k, yn).wait_recv()
        out[:, k * cols : (k + 1) * cols] = (
            own[k] + in_buf[1, k].astype(f32) + in_buf[2, k].astype(f32)
        ).astype(bf16)

    for copy in copies:
        copy.wait_send()
    for k in range(pieces):
        send(0, k, xn if k < split else yn).wait_send()
        send(1, k, xn).wait_send()
        send(2, k, yn).wait_send()

    @pl.when(has_after)
    def _():
        halo.wait_send()

    @pl.when(has_prior)
    def _():
        side_head.wait_send()
        grad_head.wait_send()

    for other in range(count):

        @pl.when(other > pos)
        def _(other=other):
            forward(pos, other).wait_send()

        @pl.when(other < pos)
        def _(other=other):
            backward(pos, other).wait_send()


def hand_over_kernel(mixed, grads, mixed_out, grads_out, sem):
    copies = [
        pltpu.make_async_copy(mixed, mixed_out, sem.at[0]),
        pltpu.make_async_copy(grads, grads_out, sem.at[1]),
    ]
    for copy in copies:
        copy.start()
    for copy in copies:
        copy.wait()


def hand_over(results):
    return pl.pallas_call(
        hand_over_kernel,
        out_shape=tuple(jax.ShapeDtypeStruct(a.shape, a.dtype) for a in results),
        in_specs=[pl.BlockSpec(memory_space=pltpu.VMEM)] * 2,
        out_specs=(pl.BlockSpec(memory_space=pl.ANY),) * 2,
        scratch_shapes=[pltpu.SemaphoreType.DMA((2,))],
        compiler_params=pltpu.CompilerParams(vmem_limit_bytes=4 * 1024 * 1024),
    )(*results)


def square_shards(tokens, in_weight, short_taps, decay_rate, residue, skip_gain, grad_out):
    count = lax.axis_size("ctx")
    rows, depth = tokens.shape
    streams, _, width = in_weight.shape
    length = 4 * rows
    modes = decay_rate.shape[0]
    tile = min(256, width)
    parts = streams * (width // tile)
    pieces = 8
    f32, bf16 = jnp.float32, jnp.bfloat16
    vmem, dma = pltpu.VMEM, pltpu.SemaphoreType.DMA
    table = vmem((modes, width), f32)
    plane = vmem((width // LANES, length, LANES), f32)
    fan = vmem((modes, SUBLANES, width), f32)
    carry = vmem((4, modes, SUBLANES, width), f32)
    ends = vmem((4, modes, width), f32)
    travelling = vmem((3, pieces, rows, depth // pieces), bf16)
    inner = pl.BlockSpec(memory_space=pltpu.VMEM)
    results = pl.pallas_call(
        functools.partial(fused_kernel, count),
        out_shape=(
            pltpu.VMEM((length, width), bf16),
            pltpu.VMEM((rows, depth), bf16),
        ),
        in_specs=[pl.BlockSpec(memory_space=pl.ANY)] * 7,
        out_specs=(inner, inner),
        scratch_shapes=[
            vmem((rows, depth), bf16),
            vmem(short_taps.shape, f32),
            table, table,
            vmem((1, width), f32),
            vmem((length, width), bf16),
            vmem((parts, depth, tile), bf16),
            vmem((3, rows, depth), bf16),
            vmem((4 * TAIL, depth), bf16),
            vmem((3, parts, rows + 8, tile), f32),
            vmem((5, parts, 8, tile), f32),
            vmem((3, length + 8, width), f32),
            plane, plane, plane, plane,
            vmem((rows + 8, streams * width), f32),
            vmem((length, streams * width), bf16),
            vmem((16, width), bf16),
            vmem((8, width), f32),
            table,
            ends, fan, fan,
            vmem((count, modes, width), f32),
            carry, carry, ends, ends,
            vmem((5, modes, width), f32),
            ends,
            vmem((5, modes, width), f32),
            ends,
            vmem((modes, width), bf16),
            vmem((modes, width), bf16),
            vmem((count, modes, width), bf16),
            vmem((count, modes, width), bf16),
            table, table,
            travelling, travelling,
            vmem((pieces, rows, depth // pieces), f32),
            dma((6,)), dma((parts,)), dma((20,)), dma((20,)), dma((3,)), dma((3,)),
            dma((count,)), dma((count,)), dma((count,)), dma((count,)),
            dma((3, pieces)), dma((3, pieces)),
        ],
        compiler_params=pltpu.CompilerParams(
            collective_id=0, has_side_effects=True, vmem_limit_bytes=VMEM_LIMIT
        ),
    )(tokens, in_weight, short_taps, decay_rate, residue, skip_gain[None], grad_out)
    return hand_over(results)


def solution(mesh):
    in_specs = (
        P(("ctx", "tp"), None),
        P(None, None, "tp"),
        P(None, None, "tp"),
        P(None, "tp"),
        P(None, "tp"),
        P("tp"),
        P("ctx", "tp"),
    )
    out_specs = (P("ctx", "tp"), P(("ctx", "tp"), None))
    body = square_shards if mesh.shape["tp"] == 4 else shards
    return jax.shard_map(body, mesh=mesh, in_specs=in_specs, out_specs=out_specs, check_vma=False)
```

```python
import functools

import jax
import jax.numpy as jnp
from jax import lax
from jax.experimental import pallas as pl
from jax.experimental.pallas import tpu as pltpu
from jax.sharding import PartitionSpec as P

exact_mode = lax.Precision.HIGHEST


def from_behind(value, axis, steps):
    count = lax.axis_size(axis)
    leading, last = (max(0, -steps), min(count, count - steps))
    return lax.ppermute(value, axis, [(source, source + steps) for source in range(leading, last)])


def modal_block(signal, log_pole, residue):
    length, channels = signal.shape
    sub_len = min(64, length)
    sub_count = length // sub_len
    offsets = jnp.arange(sub_len, dtype=jnp.float32)
    sections = signal.reshape(sub_count, sub_len, channels)
    powers = jnp.exp(log_pole[:, None, :] * offsets[None, :, None])
    filter_taps = jnp.sum(residue[:, None, :] * powers, axis=0)
    lag_index = jnp.arange(sub_len)[:, None] - jnp.arange(sub_len)[None, :]
    toeplitz = jnp.where((lag_index >= 0)[:, :, None], filter_taps[jnp.maximum(lag_index, 0)], 0.0)
    within = jnp.einsum("abc,kbc->kac", toeplitz, sections, precision=exact_mode)
    to_end = jnp.exp(log_pole[:, None, :] * (sub_len - 1.0 - offsets)[None, :, None])
    end_states = jnp.einsum("nbc,kbc->nkc", to_end, sections, precision=exact_mode)
    lag_blocks = jnp.arange(sub_count + 1)[:, None] - 1 - jnp.arange(sub_count)[None, :]
    valid_lag = lag_blocks >= 0
    lag_float = (jnp.maximum(lag_blocks, 0) * sub_len).astype(jnp.float32)
    decay_table = jnp.exp(log_pole[None, None] * lag_float[:, :, None, None])
    decay_table = jnp.where(valid_lag[:, :, None, None], decay_table, 0.0)
    carried = jnp.einsum("kmnc,nmc->nkc", decay_table, end_states, precision=exact_mode)
    stepped = residue[:, None, :] * jnp.exp(log_pole[:, None, :] * (offsets[None, :, None] + 1.0))
    output = within + jnp.einsum(
        "nac,nkc->kac", stepped, carried[:, :sub_count], precision=exact_mode
    )
    return (output.reshape(length, channels), carried[:, sub_count])


def carry_term(incoming, log_pole, residue, length):
    channels = incoming.shape[1]
    sub_len = min(64, length)
    sub_count = length // sub_len
    offsets = jnp.arange(sub_len, dtype=jnp.float32)
    stepped = residue[:, None, :] * jnp.exp(log_pole[:, None, :] * (offsets[None, :, None] + 1.0))
    block_starts = (jnp.arange(sub_count) * sub_len).astype(jnp.float32)
    start_states = incoming[:, None, :] * jnp.exp(
        log_pole[:, None, :] * block_starts[None, :, None]
    )
    output = jnp.einsum("nac,nkc->kac", stepped, start_states, precision=exact_mode)
    return output.reshape(length, channels)


def shards(tokens, in_weight, short_taps, decay_rate, residue, skip_gain, grad_out):
    width = in_weight.shape[2]
    weight_cat = jnp.concatenate([in_weight[0], in_weight[1], in_weight[2]], axis=1)
    streams = jnp.dot(
        lax.all_gather(tokens, "tp", axis=0, tiled=True),
        weight_cat,
        preferred_element_type=jnp.float32,
    ).astype(jnp.bfloat16)
    length = streams.shape[0]
    tap_reach = short_taps.shape[1] - 1
    taps_cat = jnp.concatenate([short_taps[0], short_taps[1], short_taps[2]], axis=1)
    before = from_behind(streams[length - tap_reach :], "ctx", 1)
    extended = jnp.concatenate([before, streams], axis=0).astype(jnp.float32)
    short_mixed = taps_cat[0][None] * extended[tap_reach:]
    for offset in range(1, tap_reach + 1):
        short_mixed = (
            short_mixed
            + taps_cat[offset][None] * extended[tap_reach - offset : tap_reach - offset + length]
        )
    query_side = short_mixed[:, :width]
    key_side = short_mixed[:, width : 2 * width]
    value_side = short_mixed[:, 2 * width :]
    product_in = key_side * value_side
    log_pole = -decay_rate
    forward_local, forward_sum = modal_block(product_in, log_pole, residue)
    upstream = grad_out.astype(jnp.float32)
    conv_grad = upstream * query_side
    backward_local, backward_sum = modal_block(conv_grad[::-1], log_pole, residue)
    position = lax.axis_index("ctx")
    summaries = (
        lax.all_gather(forward_sum[None], "ctx", axis=0, tiled=True),
        lax.all_gather(backward_sum[None], "ctx", axis=0, tiled=True),
    )
    block_index = jnp.arange(summaries[0].shape[0])
    earlier_gap = position - 1 - block_index
    later_gap = block_index - position - 1
    scale_fwd = (jnp.maximum(earlier_gap, 0) * length).astype(jnp.float32)
    scale_bwd = (jnp.maximum(later_gap, 0) * length).astype(jnp.float32)
    weight_fwd = jnp.where(
        (earlier_gap >= 0)[:, None, None], jnp.exp(log_pole[None] * scale_fwd[:, None, None]), 0.0
    )
    weight_bwd = jnp.where(
        (later_gap >= 0)[:, None, None], jnp.exp(log_pole[None] * scale_bwd[:, None, None]), 0.0
    )
    incoming_fwd = jnp.sum(weight_fwd * summaries[0], axis=0)
    incoming_bwd = jnp.sum(weight_bwd * summaries[1], axis=0)
    conv_out = forward_local + carry_term(incoming_fwd, log_pole, residue, length)
    back_conv = (backward_local + carry_term(incoming_bwd, log_pole, residue, length))[::-1]
    filtered = conv_out + skip_gain[None] * product_in
    result = (query_side * filtered).astype(jnp.bfloat16)
    grad_query = upstream * filtered
    grad_product = back_conv + skip_gain[None] * conv_grad
    stream_grads = jnp.concatenate(
        [grad_query, grad_product * value_side, grad_product * key_side], axis=1
    )
    after_rows = from_behind(stream_grads[:tap_reach], "ctx", -1)
    padded = jnp.concatenate([stream_grads, after_rows], axis=0)
    grad_streams = taps_cat[0][None] * padded[:length]
    for offset in range(1, tap_reach + 1):
        grad_streams = grad_streams + taps_cat[offset][None] * padded[offset : offset + length]
    grad_streams = grad_streams.astype(jnp.bfloat16)
    input_grad = lax.psum_scatter(
        jnp.einsum("rk,dk->rd", grad_streams, weight_cat, preferred_element_type=jnp.float32),
        "tp",
        scatter_dimension=0,
        tiled=True,
    )
    return (result, input_grad.astype(jnp.bfloat16))


MESH = pl.DeviceIdType.MESH
SUBLANES = 8
LANES = 128
ROWS = 32
TAIL = 16
VMEM_LIMIT = 60 * 1024 * 1024


def square_partners():
    me = lax.axis_index("tp")
    y, x = me // 2, me % 2
    return me, y * 2 + (1 - x), (1 - y) * 2 + x, (1 - y) * 2 + (1 - x)


def tree_sum(values):
    while len(values) > 1:
        values = [a + b for a, b in zip(values[::2], values[1::2])] + (
            [values[-1]] if len(values) % 2 else []
        )
    return values[0]


def fused_kernel(
    count, tok_hbm, w_hbm, taps_hbm, rate_hbm, res_hbm, skip_hbm, grad_hbm, mixed, out,
    tok, taps, rate, res, skip, grad, w_buf, held, acc, edge, side, prod, cgrad, conv, back, sgrad, gs, ghead, hrow,
    pole, dsec, dsub_f, dsub_b, gaps, carry_f, carry_b, end_f, end_b, in_f, in_b, new_f, new_b,
    mine_f, mine_b, all_f, all_b, inc_f, inc_b, out_buf, in_buf, own,
    in_sem, w_sem, ag_send, ag_recv, nb_send, nb_recv, send_f, recv_f, send_b, recv_b, rs_send, rs_recv,
):
    f32, bf16 = jnp.float32, jnp.bfloat16
    rows, depth = tok_hbm.shape
    parts, _, tile = w_buf.shape
    width = grad.shape[1]
    length = grad.shape[0]
    modes = rate.shape[0]
    per_stream = width // tile
    section = rows // SUBLANES
    tiles = width // LANES
    tail, half, quarter, eighth = rows - TAIL, depth // 2, depth // 4, depth // 8
    me, xn, yn, dg = square_partners()
    pos = lax.axis_index("ctx")

    barrier = pltpu.get_barrier_semaphore()
    for partner in (xn, yn):
        pl.semaphore_signal(barrier, inc=1, device_id={"tp": partner}, device_id_type=MESH)
    for step in range(1, count):
        pl.semaphore_signal(
            barrier, inc=1, device_id={"ctx": lax.rem(pos + step, count)}, device_id_type=MESH
        )

    pairs = (
        (rate_hbm, rate), (res_hbm, res), (taps_hbm, taps), (skip_hbm, skip),
        (tok_hbm, tok.at[pl.ds(0, rows)]), (grad_hbm, grad),
    )
    inputs = [
        pltpu.make_async_copy(source, target, in_sem.at[index])
        for index, (source, target) in enumerate(pairs)
    ]
    for load in inputs:
        load.start()
    loads = []
    for part in range(parts):
        stream, col = divmod(part, per_stream)
        load = pltpu.make_async_copy(
            w_hbm.at[stream, :, pl.ds(col * tile, tile)], w_buf.at[part], w_sem.at[part]
        )
        load.start()
        loads.append(load)

    def gather(index, source, slot, row, row_count, col, col_count, partner):
        place = (pl.ds(row, row_count), pl.ds(col, col_count))
        return pltpu.make_async_remote_copy(
            src_ref=source.at[place],
            dst_ref=held.at[(slot,) + place],
            send_sem=ag_send.at[index],
            recv_sem=ag_recv.at[index],
            device_id={"tp": partner},
            device_id_type=MESH,
        )

    from_x, from_y = held.at[0], held.at[1]
    copies = [
        gather(0, tok_hbm, 0, tail, TAIL, 0, depth, xn),
        gather(1, tok_hbm, 1, tail, TAIL, 0, depth, yn),
        gather(2, tok_hbm, 0, 0, tail, half, eighth, xn),
        gather(3, tok_hbm, 1, 0, tail, 0, eighth, yn),
        gather(4, tok_hbm, 0, 0, tail, half + eighth, eighth, xn),
        gather(5, tok_hbm, 1, 0, tail, eighth, eighth, yn),
        gather(6, tok_hbm, 0, 0, tail, 0, quarter, xn),
        gather(7, tok_hbm, 1, 0, tail, half, quarter, yn),
        gather(8, tok_hbm, 0, 0, tail, half + quarter, quarter, xn),
        gather(9, tok_hbm, 1, 0, tail, quarter, quarter, yn),
        gather(10, tok_hbm, 0, 0, tail, quarter, quarter, xn),
        gather(11, tok_hbm, 1, 0, tail, half + quarter, quarter, yn),
        gather(12, from_y, 2, tail, TAIL, 0, half, xn),
        gather(13, from_x, 2, tail, TAIL, half, half, yn),
    ]
    sixteenth = eighth // 2
    cuts = [
        (0, quarter), (quarter, eighth),
        (quarter + eighth, sixteenth), (half - sixteenth, sixteenth),
    ]
    for i, (start, size) in enumerate(cuts):
        copies.append(gather(14 + 2 * i, from_y, 2, 0, tail, start, size, xn))
        copies.append(gather(15 + 2 * i, from_x, 2, 0, tail, half + start, size, yn))

    def to_ctx(index, source, target, partner):
        return pltpu.make_async_remote_copy(
            src_ref=source,
            dst_ref=target,
            send_sem=nb_send.at[index],
            recv_sem=nb_recv.at[index],
            device_id={"ctx": partner},
            device_id_type=MESH,
        )

    after, prior = lax.rem(pos + 1, count), lax.rem(pos + count - 1, count)
    halo = to_ctx(0, edge.at[4], edge.at[0], after)
    side_head = to_ctx(
        1, side.at[:, pl.ds(0, 8), :], side.at[:, pl.ds(length, 8), :], prior
    )
    grad_head = to_ctx(2, grad_hbm.at[pl.ds(0, 16), :], ghead, prior)
    has_after, has_prior = pos < count - 1, pos > 0

    pl.semaphore_wait(barrier, 2 + count - 1)
    for index in range(4):
        copies[index].start()

    @pl.when(has_prior)
    def _():
        grad_head.start()

    @pl.when(jnp.logical_not(has_prior))
    def _():
        edge[0] = jnp.zeros((parts, 8, tile), f32)

    @pl.when(jnp.logical_not(has_after))
    def _():
        ghead[...] = jnp.zeros_like(ghead)
        side[:, pl.ds(length, 8), :] = jnp.zeros((3, 8, width), f32)

    for load in inputs:
        load.wait()
    pole[...] = jnp.exp(-rate[...])
    for index, steps in enumerate((section, 2 * section, 4 * section, rows)):
        dsec[index] = jnp.exp(rate[...] * (-1.0 * steps))
    sub = lax.broadcasted_iota(jnp.int32, (SUBLANES, LANES), 0)
    subf = lax.broadcasted_iota(jnp.int32, (SUBLANES, width), 0).astype(f32)

    @pl.loop(0, modes)
    def _(n):
        line = rate[pl.ds(n, 1), :]
        dsub_f[n] = jnp.exp(line * (subf * (-1.0 * section)))
        dsub_b[n] = jnp.exp(line * ((SUBLANES - 1.0 - subf) * (-1.0 * section)))

    @pl.loop(0, count)
    def _(g):
        gaps[g] = jnp.exp(rate[...] * (g * (-1 * length)).astype(f32))

    copies[0].wait_recv()
    copies[1].wait_recv()
    copies[12].start()
    copies[13].start()
    for index in range(4, 8):
        copies[index].start()

    def rounded(value):
        return value.astype(bf16).astype(f32)

    def multiply(slot, first, last, *ranges):
        @pl.loop(0, parts)
        def _(part):
            value = None
            for source, start, size in ranges:
                term = jnp.dot(
                    source[:, start : start + size],
                    w_buf[part, start : start + size, :],
                    preferred_element_type=f32,
                )
                value = term if value is None else value + term
            if not first:
                value = acc[slot, part, 8:, :] + value
            acc[slot, part, 8:, :] = rounded(value) if last else value

    copies[12].wait_recv()
    copies[13].wait_recv()
    for slot in range(3):
        tok[rows + slot * TAIL : rows + (slot + 1) * TAIL] = held[slot, tail:, :]
    for load in loads:
        load.wait()
    copies[8].start()
    copies[9].start()

    @pl.loop(0, parts)
    def _(part):
        value = rounded(jnp.dot(tok[...], w_buf[part], preferred_element_type=f32))
        acc[2, part, 8:, :] = value[:rows]
        for slot, owner in enumerate((me, xn, yn, dg)):
            end = rows + slot * TAIL
            edge[owner + 1, part] = value[end - 8 : end]

    @pl.when(has_after)
    def _():
        halo.start()

    @pl.when(has_prior)
    def _():
        halo.wait_recv()

    def wide(ref, lanes):
        return [
            jnp.broadcast_to(ref[n : n + 1, lanes], (SUBLANES, LANES)) for n in range(modes)
        ]

    def process(slot, owner):
        base = pl.multiple_of(owner * rows, rows)
        acc[slot, :, 0:8, :] = edge[owner]

        @pl.loop(0, rows // ROWS)
        def _(step):
            start = pl.multiple_of(step * ROWS, ROWS)
            place = pl.ds(pl.multiple_of(base + start, ROWS), ROWS)
            for col in range(0, width, LANES):
                lanes = slice(col, col + LANES)
                mixed_side = []
                for s in range(3):
                    part, inner = s * per_stream + col // tile, col % tile
                    block = acc[slot, part, pl.ds(start, ROWS + 8), inner : inner + LANES]
                    value = taps[s, 0:1, lanes] * block[8:]
                    for j in range(1, 3):
                        value = value + taps[s, j : j + 1, lanes] * block[8 - j : 8 - j + ROWS]
                    side[s, place, lanes] = value
                    mixed_side.append(value)
                prod[col // LANES, place, :] = mixed_side[1] * mixed_side[2]
                cgrad[col // LANES, place, :] = grad[place, lanes].astype(f32) * mixed_side[0]

        @pl.when(jnp.logical_and(owner == 0, has_prior))
        def _():
            side_head.start()

        @pl.loop(0, tiles)
        def _(t):
            lanes = pl.ds(pl.multiple_of(t * LANES, LANES), LANES)
            p = wide(pole, lanes)

            def body(j, state):
                fwd, bwd = state
                x = prod[t, pl.ds(base + j, SUBLANES, stride=section), :]
                y = cgrad[t, pl.ds(base + (section - 1 - j), SUBLANES, stride=section), :]
                return (
                    [a * b + x for a, b in zip(p, fwd)],
                    [a * b + y for a, b in zip(p, bwd)],
                )

            zero = [jnp.zeros((SUBLANES, LANES), f32)] * modes
            fwd, bwd = lax.fori_loop(0, section, body, (zero, zero), unroll=2)
            for n in range(modes):
                residue = res[n : n + 1, lanes]
                ahead, behind = fwd[n] * residue, bwd[n] * residue
                for index, k in enumerate((1, 2, 4)):
                    decay = dsec[index, n : n + 1, lanes]
                    ahead = ahead + jnp.where(sub >= k, decay * pltpu.roll(ahead, k, 0), 0.0)
                    behind = behind + jnp.where(
                        sub < SUBLANES - k, decay * pltpu.roll(behind, SUBLANES - k, 0), 0.0
                    )
                carry_f[owner, n, :, lanes] = jnp.where(sub >= 1, pltpu.roll(ahead, 1, 0), 0.0)
                carry_b[owner, n, :, lanes] = jnp.where(
                    sub < SUBLANES - 1, pltpu.roll(behind, SUBLANES - 1, 0), 0.0
                )
                end_f[owner, n : n + 1, lanes] = ahead[SUBLANES - 1 :]
                end_b[owner, n : n + 1, lanes] = behind[0:1]

    def scan(base, owner, source, target, carry, incoming, shrink, reverse):
        @pl.loop(0, tiles)
        def _(t):
            lanes = pl.ds(pl.multiple_of(t * LANES, LANES), LANES)
            p, r = wide(pole, lanes), wide(res, lanes)

            def body(i, state):
                j = section - 1 - i if reverse else i
                place = pl.ds(base + j, SUBLANES, stride=section)
                x = source[t, place, :]
                state = [a * b + c * x for a, b, c in zip(p, state, r)]
                target[t, place, :] = tree_sum(state)
                return state

            start = [
                carry[owner, n, :, lanes]
                + shrink[n, :, lanes] * incoming[owner, n : n + 1, lanes]
                for n in range(modes)
            ]
            lax.fori_loop(0, section, body, start, unroll=2)

    def finish_scan(owner):
        base = pl.multiple_of(owner * rows, rows)
        scan(base, owner, prod, conv, carry_f, in_f, dsub_f, False)
        scan(base, owner, cgrad, back, carry_b, in_b, dsub_b, True)

    def add_arrived(owner, target, incoming, shrink, reverse):
        base = pl.multiple_of(owner * rows, rows)

        @pl.loop(0, tiles)
        def _(t):
            lanes = pl.ds(pl.multiple_of(t * LANES, LANES), LANES)
            p = wide(pole, lanes)

            def body(i, state):
                j = section - 1 - i if reverse else i
                place = pl.ds(base + j, SUBLANES, stride=section)
                state = [a * b for a, b in zip(p, state)]
                target[t, place, :] = target[t, place, :] + tree_sum(state)
                return state

            start = [
                shrink[n, :, lanes] * incoming[owner, n : n + 1, lanes] for n in range(modes)
            ]
            lax.fori_loop(0, section, body, start, unroll=2)

    def multiply_pair(first, *ranges):
        @pl.loop(0, parts)
        def _(part):
            value = None
            for start, size in ranges:
                both = held[0:2, :, start : start + size].reshape(2 * rows, size)
                term = jnp.dot(
                    both, w_buf[part, start : start + size, :], preferred_element_type=f32
                )
                value = term if value is None else value + term
            for slot in range(2):
                here = value[slot * rows : (slot + 1) * rows]
                acc[slot, part, 8:, :] = (
                    here if first else rounded(acc[slot, part, 8:, :] + here)
                )

    copies[10].start()
    copies[11].start()
    process(2, me)
    for index in (2, 4):
        copies[index].wait_recv()
    copies[15].start()
    for index in (3, 5):
        copies[index].wait_recv()
    copies[14].start()
    for index in (6, 7):
        copies[index].wait_recv()
    multiply_pair(True, (0, quarter), (half, quarter))
    copies[8].wait_recv()
    copies[17].start()
    copies[9].wait_recv()
    copies[16].start()
    for index in (10, 11):
        copies[index].wait_recv()
    multiply_pair(False, (quarter, quarter), (half + quarter, quarter))
    copies[18].start()
    copies[19].start()
    process(0, xn)
    process(1, yn)
    copies[20].start()
    copies[21].start()
    opposite = held.at[2]
    for i, (start, size) in enumerate(cuts):
        copies[14 + 2 * i].wait_recv()
        copies[15 + 2 * i].wait_recv()
        multiply(
            2, i == 0, i == len(cuts) - 1, (opposite, start, size), (opposite, half + start, size)
        )
    process(2, dg)

    per_block = dsec[3]
    in_f[0] = jnp.zeros((modes, width), f32)
    in_b[3] = jnp.zeros((modes, width), f32)
    for block in range(4):
        in_f[block + 1] = per_block * in_f[block] + end_f[block]
    for block in (3, 2, 1):
        in_b[block - 1] = per_block * in_b[block] + end_b[block]
    mine_f[...] = in_f[4].astype(bf16)
    mine_b[...] = (per_block * in_b[0] + end_b[0]).astype(bf16)

    def summary(mine, table, send_sem, recv_sem, source, partner):
        return pltpu.make_async_remote_copy(
            src_ref=mine,
            dst_ref=table.at[source],
            send_sem=send_sem.at[partner],
            recv_sem=recv_sem.at[source],
            device_id={"ctx": partner},
            device_id_type=MESH,
        )

    forward = functools.partial(summary, mine_f, all_f, send_f, recv_f)
    backward = functools.partial(summary, mine_b, all_b, send_b, recv_b)
    for step in range(count):
        last = count - 1 - step

        @pl.when(last > pos)
        def _(last=last):
            forward(pos, last).start()

        @pl.when(step < pos)
        def _(step=step):
            backward(pos, step).start()

    finish_scan(dg)

    @pl.when(has_after)
    def _():
        grad_head.wait_recv()
        side_head.wait_recv()

    inc_f[...] = jnp.zeros_like(inc_f)
    inc_b[...] = jnp.zeros_like(inc_b)
    for other in range(count):

        @pl.when(other < pos)
        def _(other=other):
            forward(other, pos).wait_recv()
            inc_f[...] += gaps[pos - 1 - other] * all_f[other].astype(f32)

        @pl.when(other > pos)
        def _(other=other):
            backward(other, pos).wait_recv()
            inc_b[...] += gaps[other - pos - 1] * all_b[other].astype(f32)

    arrived = inc_f[...]
    for block in range(5):
        in_f[block] = in_f[block] + arrived
        new_f[block] = arrived
        arrived = arrived * per_block
    arrived = inc_b[...]
    for block in (3, 2, 1, 0):
        in_b[block] = in_b[block] + arrived
        new_b[block] = arrived
        arrived = arrived * per_block
    add_arrived(dg, conv, new_f, dsub_f, False)
    add_arrived(dg, back, new_b, dsub_b, True)

    def heads(owner):
        @pl.when(owner == 3)
        def _():
            hrow[...] = ghead[...].astype(f32)[0:8]

        @pl.when(owner < 3)
        def _():
            hrow[...] = grad[pl.ds(pl.multiple_of((owner + 1) * rows, rows), 16), :].astype(f32)[0:8]

        place = pl.ds(pl.multiple_of((owner + 1) * rows, rows), 8)
        for col in range(0, width, LANES):
            lanes = slice(col, col + LANES)
            q, k, v = (side[s, place, lanes] for s in range(3))
            g = hrow[:, lanes]
            x, cg = k * v, g * q
            p, r = pole[:, lanes], res[:, lanes]
            ahead, behind = p * in_f[owner + 1, :, lanes], in_b[owner, :, lanes]

            def total(value):
                return jnp.sum(value, axis=0, keepdims=True)

            first = sub == 0
            conv_head = jnp.where(first, total(ahead), total(p * ahead) + total(r * p) * x[0:1])
            conv_head = conv_head + total(r) * x
            back_head = jnp.where(
                first, total(behind), total(behind / p) - total(r / p) * cg[0:1]
            )
            gain = skip[0:1, lanes]
            filtered = conv_head + gain * x
            product = back_head + gain * cg
            for s, value in enumerate((g * filtered, product * v, product * k)):
                sgrad[rows:, s * width + col : s * width + col + LANES] = value

    def finish_block(owner):
        base = pl.multiple_of(owner * rows, rows)
        heads(owner)

        @pl.loop(0, rows // ROWS)
        def _(step):
            start = pl.multiple_of(step * ROWS, ROWS)
            here = pl.ds(start, ROWS)
            place = pl.ds(pl.multiple_of(base + start, ROWS), ROWS)
            for col in range(0, width, LANES):
                lanes = slice(col, col + LANES)
                gain = skip[0:1, lanes]
                filtered = conv[col // LANES, place, :] + gain * prod[col // LANES, place, :]
                mixed[place, lanes] = (side[0, place, lanes] * filtered).astype(bf16)
                product = back[col // LANES, place, :] + gain * cgrad[col // LANES, place, :]
                upstream = grad[place, lanes].astype(f32)
                sgrad[here, lanes] = upstream * filtered
                sgrad[here, width + col : width + col + LANES] = product * side[2, place, lanes]
                sgrad[here, 2 * width + col : 2 * width + col + LANES] = (
                    product * side[1, place, lanes]
                )

        @pl.loop(0, rows // ROWS)
        def _(step):
            start = pl.multiple_of(step * ROWS, ROWS)
            place = pl.ds(pl.multiple_of(base + start, ROWS), ROWS)
            for s in range(3):
                for col in range(0, width, LANES):
                    lanes = slice(s * width + col, s * width + col + LANES)
                    block = sgrad[pl.ds(start, ROWS + 8), lanes]
                    value = taps[s, 0:1, col : col + LANES] * block[:ROWS]
                    for j in range(1, 3):
                        value = value + taps[s, j : j + 1, col : col + LANES] * block[j : j + ROWS]
                    gs[place, lanes] = value.astype(bf16)

    _, pieces, _, cols = out_buf.shape
    split = pieces // 2

    def send(kind, piece, partner):
        return pltpu.make_async_remote_copy(
            src_ref=out_buf.at[kind, piece],
            dst_ref=in_buf.at[kind, piece],
            send_sem=rs_send.at[kind, piece],
            recv_sem=rs_recv.at[kind, piece],
            device_id={"tp": partner},
            device_id_type=MESH,
        )

    def partial(owner, piece):
        block = pl.ds(pl.multiple_of(owner * rows, rows), rows)
        here = pl.ds(pl.multiple_of(piece * cols, cols), cols)
        total = None
        for part in range(parts):
            term = lax.dot_general(
                gs[block, part * tile : (part + 1) * tile],
                w_buf[part, here, :],
                (((1,), (1,)), ((), ())),
                preferred_element_type=f32,
            )
            total = term if total is None else total + term
        return total

    def emit(kind, piece, value, partner):
        out_buf[kind, piece] = value.astype(bf16)
        send(kind, piece, partner).start()

    finish_block(dg)

    @pl.loop(0, split)
    def _(k):
        emit(0, k, partial(dg, k), xn)
        emit(0, split + k, partial(dg, split + k), yn)

    finish_scan(xn)
    finish_block(xn)
    finish_scan(yn)
    finish_block(yn)

    @pl.loop(0, split)
    def _(k):
        emit(1, k, partial(xn, k), xn)
        emit(2, split + k, partial(yn, split + k), yn)

    @pl.loop(0, split)
    def _(k):
        own_x, own_y = partial(xn, split + k), partial(yn, k)
        send(0, split + k, yn).wait_recv()
        emit(1, split + k, own_x + in_buf[0, split + k].astype(f32), xn)
        send(0, k, xn).wait_recv()
        emit(2, k, own_y + in_buf[0, k].astype(f32), yn)

    finish_scan(me)
    finish_block(me)

    @pl.loop(0, pieces)
    def _(k):
        own[k] = partial(me, k)

    for k in [k + offset for k in range(split) for offset in (0, split)]:
        send(1, k, xn).wait_recv()
        send(2, k, yn).wait_recv()
        out[:, k * cols : (k + 1) * cols] = (
            own[k] + in_buf[1, k].astype(f32) + in_buf[2, k].astype(f32)
        ).astype(bf16)

    for copy in copies:
        copy.wait_send()
    for k in range(pieces):
        send(0, k, xn if k < split else yn).wait_send()
        send(1, k, xn).wait_send()
        send(2, k, yn).wait_send()

    @pl.when(has_after)
    def _():
        halo.wait_send()

    @pl.when(has_prior)
    def _():
        side_head.wait_send()
        grad_head.wait_send()

    for other in range(count):

        @pl.when(other > pos)
        def _(other=other):
            forward(pos, other).wait_send()

        @pl.when(other < pos)
        def _(other=other):
            backward(pos, other).wait_send()


def hand_over_kernel(mixed, grads, mixed_out, grads_out, sem):
    copies = [
        pltpu.make_async_copy(mixed, mixed_out, sem.at[0]),
        pltpu.make_async_copy(grads, grads_out, sem.at[1]),
    ]
    for copy in copies:
        copy.start()
    for copy in copies:
        copy.wait()


def hand_over(results):
    return pl.pallas_call(
        hand_over_kernel,
        out_shape=tuple(jax.ShapeDtypeStruct(a.shape, a.dtype) for a in results),
        in_specs=[pl.BlockSpec(memory_space=pltpu.VMEM)] * 2,
        out_specs=(pl.BlockSpec(memory_space=pl.ANY),) * 2,
        scratch_shapes=[pltpu.SemaphoreType.DMA((2,))],
        compiler_params=pltpu.CompilerParams(vmem_limit_bytes=4 * 1024 * 1024),
    )(*results)


def square_shards(tokens, in_weight, short_taps, decay_rate, residue, skip_gain, grad_out):
    count = lax.axis_size("ctx")
    rows, depth = tokens.shape
    streams, _, width = in_weight.shape
    length = 4 * rows
    modes = decay_rate.shape[0]
    tile = min(256, width)
    parts = streams * (width // tile)
    pieces = 8
    f32, bf16 = jnp.float32, jnp.bfloat16
    vmem, dma = pltpu.VMEM, pltpu.SemaphoreType.DMA
    table = vmem((modes, width), f32)
    plane = vmem((width // LANES, length, LANES), f32)
    fan = vmem((modes, SUBLANES, width), f32)
    carry = vmem((4, modes, SUBLANES, width), f32)
    ends = vmem((4, modes, width), f32)
    travelling = vmem((3, pieces, rows, depth // pieces), bf16)
    inner = pl.BlockSpec(memory_space=pltpu.VMEM)
    results = pl.pallas_call(
        functools.partial(fused_kernel, count),
        out_shape=(
            pltpu.VMEM((length, width), bf16),
            pltpu.VMEM((rows, depth), bf16),
        ),
        in_specs=[pl.BlockSpec(memory_space=pl.ANY)] * 7,
        out_specs=(inner, inner),
        scratch_shapes=[
            vmem((rows + 3 * TAIL, depth), bf16),
            vmem(short_taps.shape, f32),
            table, table,
            vmem((1, width), f32),
            vmem((length, width), bf16),
            vmem((parts, depth, tile), bf16),
            vmem((3, rows, depth), bf16),
            vmem((3, parts, rows + 8, tile), f32),
            vmem((5, parts, 8, tile), f32),
            vmem((3, length + 8, width), f32),
            plane, plane, plane, plane,
            vmem((rows + 8, streams * width), f32),
            vmem((length, streams * width), bf16),
            vmem((16, width), bf16),
            vmem((8, width), f32),
            table,
            ends, fan, fan,
            vmem((count, modes, width), f32),
            carry, carry, ends, ends,
            vmem((5, modes, width), f32),
            ends,
            vmem((5, modes, width), f32),
            ends,
            vmem((modes, width), bf16),
            vmem((modes, width), bf16),
            vmem((count, modes, width), bf16),
            vmem((count, modes, width), bf16),
            table, table,
            travelling, travelling,
            vmem((pieces, rows, depth // pieces), f32),
            dma((6,)), dma((parts,)), dma((22,)), dma((22,)), dma((3,)), dma((3,)),
            dma((count,)), dma((count,)), dma((count,)), dma((count,)),
            dma((3, pieces)), dma((3, pieces)),
        ],
        compiler_params=pltpu.CompilerParams(
            collective_id=0, has_side_effects=True, vmem_limit_bytes=VMEM_LIMIT
        ),
    )(tokens, in_weight, short_taps, decay_rate, residue, skip_gain[None], grad_out)
    return hand_over(results)


def solution(mesh):
    in_specs = (
        P(("ctx", "tp"), None),
        P(None, None, "tp"),
        P(None, None, "tp"),
        P(None, "tp"),
        P(None, "tp"),
        P("tp"),
        P("ctx", "tp"),
    )
    out_specs = (P("ctx", "tp"), P(("ctx", "tp"), None))
    body = square_shards if mesh.shape["tp"] == 4 else shards
    return jax.shard_map(body, mesh=mesh, in_specs=in_specs, out_specs=out_specs, check_vma=False)
```
